32 devices in a mesh: space: 4 (over z), tins: 4 (over y, core), tsink: 2 (over x).
Axes of the slice: x: 2, y: 2, z: 4, core: 2. Of those that a mesh axis runs over, the one named last changes fastest.
Arguments:
- eigvecs: float32 [4, 2, 3, 128, 16, 256], P('tins', None, None, 'tsink', 'space'), may hold values from -0.375 to 0.375
- links: float32 [4, 3, 2, 3, 3, 16, 256], P('tins', None, None, None, None, 'space'), may hold values from -3.5 to 3.5
- momenta: int32 [2, 3], replicated, may hold values from -2 to 2
- directions: int32 [3], replicated, may hold values from 0 to 2
- ins_time: int32 [4], P('tins'), may hold values from 0 to 3, as said below
- sink_time: int32 [2], P('tsink'), may hold values from 1 to 4
- sink_peramb: float32 [2, 4, 2, 512, 512], P('tsink', 'tins', None, 'space'), may hold values from -0.375 to 0.375
- source_peramb: float32 [4, 2, 512, 512], P('tins'), may hold values from -0.1875 to 0.1875
Outputs:
- gen_peramb: float32 [512, 2, 6, 2, 512], P('tins', 'tsink', None, None, 'space')
The draws below stay inside these ranges and needn't reach their ends.
Inputs may be any that keep to these rules, and one draw needn't show every extreme that they name: `ins_time`: each lattice timeslice of the window appears in exactly one slot. `sink_time`: sink timeslices on the numbering of ins_time. `momenta`: momentum components in units of 2 pi / 16. `directions`: 0 is x, 1 is y, 2 is z.
All inputs are finite; a program needn't handle non-finite values.
Results may differ from the reference program's by a relative error of at most 0.0003.
Values sent between devices are 32-bit elements; how exact they have to be, the bound alone decides.
A program may use at most 64 MiB of HBM per device.

```python
import math
import jax
import jax.numpy as jnp
from jax import lax

L = 16
PLANE = 256
NV = 128
NSPIN = 4
M = 512
NMOM = 2
NDISP = 3
T_INS = 4
T_SINK = 2


def draw_ins_time(key, part):
    return jax.random.permutation(jax.random.fold_in(key, 7), T_INS).astype(jnp.int32)


def touch_ends(array, own_key, least, high):
    place = [jax.random.randint(jax.random.fold_in(own_key, axis), (), 0, length) for axis, length in enumerate(array.shape)]
    longest = array.shape.index(max(array.shape))
    neighbour = place[:longest] + [(place[longest] + 1) % array.shape[longest]] + place[longest + 1:]
    return array.at[tuple(place)].set(least).at[tuple(neighbour)].set(high)


def block_levels(own_key, dims, split, least, top_value):
    loudness = 1.0
    for axis_at, shards_of in split:
        draws = jax.random.uniform(jax.random.fold_in(jax.random.fold_in(own_key, 6), axis_at), (shards_of,), jnp.float32, least / len(split), top_value / len(split))
        loudness = loudness * jnp.repeat(jnp.exp(draws), dims[axis_at] // shards_of).reshape((-1,) + (1,) * (len(dims) - 1 - axis_at))
    return loudness


def scatter_about(key, shape, deviation, limit, split=(), kind=jnp.bfloat16):
    level = block_levels(key, shape, split, -0.22, 0.18) if split else 1.0
    values = jax.random.normal(key, shape, jnp.float32) * deviation * level
    return jnp.minimum(jnp.maximum(values, -limit), limit).astype(kind)


def setup_inputs(seed: int = 0) -> dict:
    arg_keys = jax.random.split(jax.random.key(seed), 9)
    return {
        "eigvecs": scatter_about(arg_keys[0], (T_INS, 2, 3, NV, L, PLANE), (L * L) ** -0.5, 0.375, ((0, 4), (3, 2), (4, 4)), jnp.float32),
        "links": scatter_about(arg_keys[1], (T_INS, 3, 2, 3, 3, L, PLANE), 3 ** -0.5, 3.5, ((0, 4), (5, 4)), jnp.float32),
        "momenta": touch_ends(jax.random.randint(arg_keys[2], (NMOM, 3), -2, 3), jax.random.fold_in(arg_keys[2], 1), -2, 2).astype(jnp.int32),
        "directions": jax.random.randint(arg_keys[3], (NDISP,), 0, 3).astype(jnp.int32),
        "ins_time": draw_ins_time(jax.random.fold_in(arg_keys[8], 71), 0),
        "sink_time": jax.random.randint(arg_keys[5], (T_SINK,), 1, T_INS + 1).astype(jnp.int32),
        "sink_peramb": scatter_about(arg_keys[6], (T_SINK, T_INS, 2, M, M), (2 * NV) ** -0.5, 0.375, ((0, 2), (1, 4), (3, 4)), jnp.float32),
        "source_peramb": scatter_about(arg_keys[7], (T_INS, 2, M, M), (2 * M) ** -0.5, 0.1875, ((0, 4),), jnp.float32),
    }


HIGHEST = lax.Precision.HIGHEST


def plane_shift(source, axis_dir, step_sign, side_len):
    if axis_dir == 1:
        return jnp.roll(source, -step_sign * side_len, axis=-1)
    column = lax.broadcasted_iota(jnp.int32, (side_len * side_len,), 0) % side_len
    if step_sign == 1:
        return jnp.where(column == side_len - 1, jnp.roll(source, side_len - 1, axis=-1), jnp.roll(source, -1, axis=-1))
    return jnp.where(column == 0, jnp.roll(source, 1 - side_len, axis=-1), jnp.roll(source, 1, axis=-1))


def color_apply(link_mat, vector, adjoint):
    link_re, link_im = link_mat[:, 0], link_mat[:, 1]
    vec_re, vec_im = vector[:, 0], vector[:, 1]
    rows_real = []
    rows_imag = []
    for colour in range(3):
        sum_real = jnp.zeros_like(vec_re[:, 0])
        sum_imag = jnp.zeros_like(vec_re[:, 0])
        for inner in range(3):
            if adjoint:
                here_re = link_re[:, inner, colour][:, None]
                here_im = -link_im[:, inner, colour][:, None]
            else:
                here_re = link_re[:, colour, inner][:, None]
                here_im = link_im[:, colour, inner][:, None]
            sum_real = sum_real + here_re * vec_re[:, inner] - here_im * vec_im[:, inner]
            sum_imag = sum_imag + here_re * vec_im[:, inner] + here_im * vec_re[:, inner]
        rows_real.append(sum_real)
        rows_imag.append(sum_imag)
    return jnp.stack([jnp.stack(rows_real, axis=1), jnp.stack(rows_imag, axis=1)], axis=1)


def covariant(link_here, link_below, vec_above, vec_below):
    return color_apply(link_here, vec_above, False) - color_apply(link_below, vec_below, True)


def plane_derivs(vectors, link_all, side_len):
    result = []
    for axis_dir in range(2):
        link_here = link_all[:, axis_dir]
        vec_above = plane_shift(vectors, axis_dir, 1, side_len)
        vec_below = plane_shift(vectors, axis_dir, -1, side_len)
        link_below = plane_shift(link_here, axis_dir, -1, side_len)
        result.append(covariant(link_here, link_below, vec_above, vec_below))
    return result


def phase_factors(momenta, z_coord, side_len):
    site_index = lax.broadcasted_iota(jnp.int32, (side_len * side_len,), 0)
    x_coord = site_index % side_len
    y_coord = site_index // side_len
    product = (momenta[:, 0, None, None] * x_coord[None, None, :]
               + momenta[:, 1, None, None] * y_coord[None, None, :]
               + momenta[:, 2, None, None] * z_coord[None, :, None])
    angles = (2.0 * math.pi / side_len) * jnp.mod(product, side_len).astype(jnp.float32)
    return jnp.cos(angles), jnp.sin(angles)


def phase_kets(derivative, directions, momenta, z_coord, side_len):
    onehot = (directions[:, None] == jnp.arange(3, dtype=jnp.int32)[None, :]).astype(jnp.float32)
    chosen = jnp.zeros((derivative.shape[1], onehot.shape[0]) + derivative.shape[2:], jnp.float32)
    for axis_dir in range(3):
        chosen = chosen + onehot[None, :, axis_dir, None, None, None, None, None] * derivative[axis_dir][:, None]
    cos_part, sine_part = phase_factors(momenta, z_coord, side_len)
    cos_part = cos_part[None, :, None, None, None, :, :]
    sine_part = sine_part[None, :, None, None, None, :, :]
    disp_real = chosen[:, None, :, 0]
    disp_imag = chosen[:, None, :, 1]
    wave_real = cos_part * disp_real + sine_part * disp_imag
    wave_imag = cos_part * disp_imag - sine_part * disp_real
    stacked = jnp.concatenate([wave_real, wave_imag], axis=3)
    shape_now = stacked.shape
    return stacked.reshape((shape_now[0], shape_now[1] * shape_now[2]) + shape_now[3:])


def elemental_part(bra_waves, ket_waves, pattern):
    swapped = jnp.concatenate([ket_waves[:, :, 3:], -ket_waves[:, :, :3]], axis=2)
    real_part = jnp.einsum(pattern, bra_waves, ket_waves, precision=HIGHEST)
    imag_part = jnp.einsum(pattern, bra_waves, swapped, precision=HIGHEST)
    return jnp.stack([real_part, imag_part], axis=2)


def left_product(row_block, elemental, weight):
    count_t = row_block.shape[0]
    row_count = row_block.shape[2]
    order_m = row_block.shape[3]
    split_rows = row_block.reshape(count_t, 2, row_count, NSPIN, order_m // NSPIN)
    rows_re, rows_im = split_rows[:, 0], split_rows[:, 1]
    elem_re, elem_im = elemental[:, :, 0], elemental[:, :, 1]

    def contract(first_op, second_op):
        return jnp.einsum("trsa,tqba->tqrsb", first_op, second_op, precision=HIGHEST)

    spin_sign = jnp.where(jnp.arange(NSPIN) < 2, 1.0, -1.0).astype(jnp.float32)
    factor = weight[:, None, None, None, None] * spin_sign[None, None, None, :, None]
    left_re = factor * (contract(rows_re, elem_re) - contract(rows_im, elem_im))
    left_im = factor * (contract(rows_re, elem_im) + contract(rows_im, elem_re))
    pairs = elemental.shape[1]
    return (left_re.reshape(count_t, pairs, row_count, order_m),
            left_im.reshape(count_t, pairs, row_count, order_m))


def right_product(left_re, left_im, src_re, src_im):
    def contract(first_op, second_op):
        return jnp.einsum("tqrk,tkc->cqr", first_op, second_op, precision=HIGHEST)

    gen_re = contract(left_re, src_re) - contract(left_im, src_im)
    gen_im = contract(left_re, src_im) + contract(left_im, src_re)
    return jnp.stack([gen_re, gen_im], axis=2)


def reference(eigvecs, links, momenta, directions, ins_time, sink_time, sink_peramb, source_peramb):
    z_coord = jnp.arange(L, dtype=jnp.int32)

    def one_time(time_pair):
        vector_t = time_pair[0][None]
        link_t = time_pair[1][None]
        derivs = plane_derivs(vector_t, link_t, L)
        link_z = link_t[:, 2]
        derivs.append(covariant(link_z, jnp.roll(link_z, 1, axis=4),
                                jnp.roll(vector_t, -1, axis=4), jnp.roll(vector_t, 1, axis=4)))
        derivative = jnp.stack(derivs)
        ket_waves = phase_kets(derivative, directions, momenta, z_coord, L)
        bra_waves = vector_t.reshape((1, 6) + vector_t.shape[3:])
        return elemental_part(bra_waves, ket_waves, "tkazp,tqkbzp->tqba")[0]

    elemental = lax.map(one_time, (eigvecs, links))
    src_re = source_peramb[:, 0]
    src_im = source_peramb[:, 1]

    def one_sink(sink_pair):
        row_block, sink_limit = sink_pair
        weight = (ins_time < sink_limit).astype(jnp.float32)
        left_re, left_im = left_product(row_block, elemental, weight)
        return right_product(left_re, left_im, src_re, src_im)

    generalized = lax.map(one_sink, (sink_peramb, sink_time))
    return jnp.moveaxis(generalized, 0, 1)
```

```python
import functools
import math

import jax
import jax.numpy as jnp
from jax import lax
from jax.experimental import pallas as pl
from jax.experimental.pallas import tpu as pltpu
from jax.sharding import PartitionSpec as P

L = 16
NSPIN = 4
BF16 = jnp.bfloat16
F32 = jnp.float32
NT = (((1,), (1,)), ((), ()))
NN = (((1,), (0,)), ((), ()))


def split(x):
    hi = x.astype(BF16)
    return hi, (x - hi.astype(F32)).astype(BF16)


def dot3(a_hi, a_lo, b_hi, b_lo, dims):
    def one(a, b):
        return lax.dot_general(a, b, dims, preferred_element_type=F32)

    return one(a_hi, b_hi) + one(a_hi, b_lo) + one(a_lo, b_hi)


def remote(src, dst, send, recv, axis, index):
    return pltpu.make_async_remote_copy(
        src_ref=src,
        dst_ref=dst,
        send_sem=send,
        recv_sem=recv,
        device_id={axis: index},
        device_id_type=pl.DeviceIdType.MESH,
    )


def colour_rows(link, vec, adjoint):
    rows = []
    for i in range(3):
        re = im = None
        for j in range(3):
            if adjoint:
                a, b = link[0][j][i], link[1][j][i]
                tr = a * vec[j] + b * vec[3 + j]
                ti = a * vec[3 + j] - b * vec[j]
            else:
                a, b = link[0][i][j], link[1][i][j]
                tr = a * vec[j] - b * vec[3 + j]
                ti = a * vec[3 + j] + b * vec[j]
            re = tr if re is None else re + tr
            im = ti if im is None else im + ti
        rows.append((re, im))
    return [r[0] for r in rows] + [r[1] for r in rows]


def ring_kernel(
    n_ts, n_sp, dir_ref, mom_ref, ins_ref, sink_ref, ev_ref, link_ref, p_ref, s_ref, out_ref,
    cos_ref, sin_ref, p_vm, s_vm, in_sem,
    bra, w_top, halo_up, halo_dn, ket_hi, ket_lo, rhs_hi, rhs_lo, acc, epart, rs_buf, e_own,
    e_full, e_hi, e_lo, st_hi, st_lo, p2_hi, p2_lo, l2_hi, l2_lo, tmp_a, recv_a, sum_a, tmp_b,
    recv_b, recv_y, loc_sem, bra_s, bra_r, halo_s, halo_r, rs_s, rs_r, ag_s, ag_r, fx_s, fx_r,
    a_s, a_r, y_s, y_r, b_s, b_r,
):
    _, vecs, depth, plane = ev_ref.shape
    pairs2 = epart.shape[0]
    pairs = pairs2 // 2
    n_dir = 3
    n_mom = pairs // n_dir
    nv = bra.shape[2]
    me_x = lax.axis_index("tsink")
    me_z = lax.axis_index("space")
    me_t = lax.axis_index("tins")
    core = me_t % 2
    mate = me_t + 1 - 2 * core
    far = (me_t + 2) % 4
    up = (me_z + 1) % n_sp
    down = (me_z + n_sp - 1) % n_sp
    my_rows = pl.ds(pl.multiple_of(me_x * vecs, vecs), vecs)
    local = [
        pltpu.make_async_copy(ev_ref.at[:, :, z, :], bra.at[z, :, my_rows, :], loc_sem.at[z])
        for z in range(depth)
    ]
    for copy in reversed(local):
        copy.start()
    load_p = pltpu.make_async_copy(p_ref, p_vm, in_sem.at[0])
    load_s = pltpu.make_async_copy(s_ref, s_vm, in_sem.at[1])
    load_p.start()
    load_s.start()
    barrier = pltpu.get_barrier_semaphore()
    mesh_type = pl.DeviceIdType.MESH
    for d in range(1, n_ts):
        pl.semaphore_signal(barrier, inc=1, device_id={"tsink": (me_x + d) % n_ts},
                            device_id_type=mesh_type)
    for d in range(1, n_sp):
        pl.semaphore_signal(barrier, inc=1, device_id={"space": (me_z + d) % n_sp},
                            device_id_type=mesh_type)
    for target in (mate, far):
        pl.semaphore_signal(barrier, inc=1, device_id={"tins": target}, device_id_type=mesh_type)
    pl.semaphore_wait(barrier, n_ts - 1 + n_sp - 1 + 2)

    order = list(range(1, depth - 1)) + [0, depth - 1]
    bra_copies = {}
    for z in order:
        bra_copies[z] = [
            remote(ev_ref.at[:, :, z, :], bra.at[z, :, my_rows, :], bra_s.at[z, d - 1], bra_r.at[z, d - 1],
                   "tsink", (me_x + d) % n_ts)
            for d in range(1, n_ts)
        ]
    halo_v = remote(ev_ref.at[:, :, 0, :], halo_up, halo_s.at[0], halo_r.at[0], "space", down)
    halo_w = remote(w_top, halo_dn, halo_s.at[1], halo_r.at[1], "space", up)
    halo_v.start()
    for z in order:
        for copy in bra_copies[z]:
            copy.start()

    block = min(16, vecs)
    n_block = vecs // block

    def rows_of(b):
        return pl.ds(pl.multiple_of(b * block, block), block)

    def own(z, c, b):
        return bra[z, c, pl.ds(pl.multiple_of(me_x * vecs + b * block, block), block), :]

    def links_at(k, z):
        return [
            [[link_ref[k, part, i, j, pl.ds(z, 1), :] for j in range(3)] for i in range(3)]
            for part in range(2)
        ]

    column = lax.broadcasted_iota(jnp.int32, (block, plane), 1) % L

    def shifted(x, k, sign):
        if k == 1:
            return pltpu.roll(x, plane - L if sign > 0 else L, axis=1)
        if sign > 0:
            return jnp.where(column == L - 1, pltpu.roll(x, L - 1, axis=1),
                             pltpu.roll(x, plane - 1, axis=1))
        return jnp.where(column == 0, pltpu.roll(x, plane + 1 - L, axis=1),
                         pltpu.roll(x, 1, axis=1))

    site = lax.broadcasted_iota(jnp.int32, (depth, plane), 1)
    z_coord = me_z * depth + lax.broadcasted_iota(jnp.int32, (depth, plane), 0)
    for m in range(n_mom):
        product = mom_ref[m, 0] * (site % L) + mom_ref[m, 1] * (site // L) + mom_ref[m, 2] * z_coord
        angles = (2.0 * math.pi / L) * jnp.bitwise_and(product, L - 1).astype(F32)
        cos_ref[m] = jnp.cos(angles)
        sin_ref[m] = jnp.sin(angles)

    def put_kets(k, z, b, deriv):
        for m in range(n_mom):
            c = cos_ref[m, pl.ds(z, 1), :]
            s = sin_ref[m, pl.ds(z, 1), :]
            start = pl.multiple_of((m * n_dir + k) * vecs + b * block, block)
            for i in range(3):
                for comp, val in (
                    (i, c * deriv[i] + s * deriv[3 + i]),
                    (3 + i, c * deriv[3 + i] - s * deriv[i]),
                ):
                    hi, lo = split(val)
                    cols = slice(comp * plane, (comp + 1) * plane)
                    ket_hi[z, pl.ds(start, block), cols] = hi
                    ket_lo[z, pl.ds(start, block), cols] = lo

    local[depth - 1].wait()

    def top_body(b, carry):
        vec = [own(depth - 1, c, b) for c in range(6)]
        w = colour_rows(links_at(2, depth - 1), vec, True)
        for c in range(6):
            w_top[c, rows_of(b), :] = w[c]
        return carry

    lax.fori_loop(0, n_block, top_body, 0)
    halo_w.start()
    for copy in local[:-1]:
        copy.wait()

    for k in range(2):
        def xy_body(t, carry, k=k):
            z = t // n_block
            b = t % n_block
            vec = [own(z, c, b) for c in range(6)]
            link = links_at(k, z)
            ahead = colour_rows(link, [shifted(x, k, 1) for x in vec], False)
            back = colour_rows(link, vec, True)
            put_kets(k, z, b, [ahead[c] - shifted(back[c], k, -1) for c in range(6)])
            return carry

        lax.fori_loop(0, depth * n_block, xy_body, 0)

    def z_planes(z, b, above, below):
        link = links_at(2, z)
        ahead = colour_rows(link, above, False)
        put_kets(2, z, b, [ahead[c] - below[c] for c in range(6)])

    def own_back(z, b):
        return colour_rows(links_at(2, z), [own(z, c, b) for c in range(6)], True)

    def mid_body(t, carry):
        z = t // n_block + 1
        b = t % n_block
        above = [own(z + 1, c, b) for c in range(6)]
        z_planes(z, b, above, own_back(z - 1, b))
        return carry

    lax.fori_loop(0, (depth - 2) * n_block, mid_body, 0)

    load_s.wait()
    load_p.wait()
    half = s_ref.shape[1]
    for part in range(2):
        def st_body(cb, carry, part=part):
            c_at = pl.multiple_of(cb * 128, 128)
            for kb in range(half // 128):
                tile = s_vm[part, kb * 128:(kb + 1) * 128, pl.ds(c_at, 128)].T
                hi, lo = split(tile)
                cols = slice(part * half + kb * 128, part * half + (kb + 1) * 128)
                st_hi[pl.ds(c_at, 128), cols] = hi
                st_lo[pl.ds(c_at, 128), cols] = lo
            return carry

        lax.fori_loop(0, half // 128, st_body, 0)
    weight = jnp.where(ins_ref[0] < sink_ref[0], 1.0, 0.0).astype(F32)
    rows = p_ref.shape[1]
    for spin in range(NSPIN):
        scale = weight if spin < 2 else -weight
        re = p_vm[0, :, spin * nv:(spin + 1) * nv] * scale
        im = p_vm[1, :, spin * nv:(spin + 1) * nv] * scale
        for row, col, val in ((0, 0, re), (0, 1, -im), (1, 0, im), (1, 1, re)):
            hi, lo = split(val)
            p2_hi[spin, row * rows:(row + 1) * rows, col * nv:(col + 1) * nv] = hi
            p2_lo[spin, row * rows:(row + 1) * rows, col * nv:(col + 1) * nv] = lo

    def elemental(z):
        for copy in bra_copies[z]:
            copy.wait_recv()
        for c in range(3):
            re_hi, re_lo = split(bra[z, c])
            im_hi, im_lo = split(bra[z, 3 + c])
            for ref, re, im in ((rhs_hi, re_hi, im_hi), (rhs_lo, re_lo, im_lo)):
                left_cols = slice(c * plane, (c + 1) * plane)
                right_cols = slice((3 + c) * plane, (4 + c) * plane)
                ref[0:nv, left_cols] = re
                ref[0:nv, right_cols] = im
                ref[nv:2 * nv, left_cols] = -im
                ref[nv:2 * nv, right_cols] = re
        part = dot3(ket_hi[z], ket_lo[z], rhs_hi[...], rhs_lo[...], NT).reshape(acc.shape)
        if z == order[0]:
            acc[...] = part
        else:
            acc[...] += part

    for z in order[:-2]:
        elemental(z)

    halo_w.wait()

    def low_body(b, carry):
        above = [own(1, c, b) for c in range(6)]
        z_planes(0, b, above, [halo_dn[c, rows_of(b), :] for c in range(6)])
        return carry

    lax.fori_loop(0, n_block, low_body, 0)
    halo_v.wait()

    def high_body(b, carry):
        above = [halo_up[c, rows_of(b), :] for c in range(6)]
        z_planes(depth - 1, b, above, own_back(depth - 2, b))
        return carry

    lax.fori_loop(0, n_block, high_body, 0)
    for z in order[-2:]:
        elemental(z)

    for m in range(n_mom):
        for e in range(n_dir):
            for part in range(2):
                epart[2 * (m * n_dir + e) + part] = acc[
                    m * n_dir + dir_ref[e], :, part * nv:(part + 1) * nv]

    n_group = pairs2 // n_sp
    per_group = n_sp // 2

    def rs_copy(g, d):
        peer = (me_z + d) % n_sp
        return remote(epart.at[g * n_sp + peer], rs_buf.at[g, d - 1], rs_s.at[g, d - 1],
                      rs_r.at[g, d - 1], "space", peer)

    def ag_copy(g, d):
        return remote(e_own.at[g], e_full.at[g * n_sp + me_z, my_rows, :], ag_s.at[g, d - 1],
                      ag_r.at[g, d - 1], "space", (me_z + d) % n_sp)

    def fx_copy(g, slot, d):
        owner = (me_z + n_sp - slot) % n_sp
        target = e_full.at[g * n_sp + owner, my_rows, :]
        return remote(target if slot else e_own.at[g], target, fx_s.at[g, slot, d - 1],
                      fx_r.at[g, slot, d - 1], "tsink", (me_x + d) % n_ts)

    def reduce(g):
        total = epart[g * n_sp + me_z]
        for d in range(1, n_sp):
            rs_copy(g, d).wait_recv()
            total = total + rs_buf[g, d - 1]
        e_own[g] = total
        e_full[g * n_sp + me_z, my_rows, :] = total
        for d in range(1, n_sp):
            ag_copy(g, d).start()
        for d in range(1, n_ts):
            fx_copy(g, 0, d).start()

    def forward(g):
        for slot in range(1, n_sp):
            ag_copy(g, slot).wait_recv()
            for d in range(1, n_ts):
                fx_copy(g, slot, d).start()

    def left(g):
        for slot in range(n_sp):
            for d in range(1, n_ts):
                fx_copy(g, slot, d).wait_recv()
        for i in range(per_group):
            for part in range(2):
                hi, lo = split(e_full[g * n_sp + 2 * i + part])
                e_hi[i * nv:(i + 1) * nv, part * nv:(part + 1) * nv] = hi
                e_lo[i * nv:(i + 1) * nv, part * nv:(part + 1) * nv] = lo

        def left_body(spin, carry):
            prod = dot3(e_hi[...], e_lo[...], p2_hi[spin], p2_lo[spin], NT)
            at = pl.ds(pl.multiple_of(spin * nv, nv), nv)
            at_low = pl.ds(pl.multiple_of(half + spin * nv, nv), nv)
            for i in range(per_group):
                hi, lo = split(prod[i * nv:(i + 1) * nv])
                for ref, val in ((l2_hi, hi), (l2_lo, lo)):
                    ref[g * per_group + i, at, :] = val
                    ref[g * per_group + i, at_low, 0:rows] = -val[:, rows:]
                    ref[g * per_group + i, at_low, rows:] = val[:, :rows]
            return carry

        lax.fori_loop(0, NSPIN, left_body, 0)

    def spread(g):
        for d in range(1, n_sp):
            rs_copy(g, d).start()

    for g in range(n_group):
        spread(g)
    n_col = recv_a.shape[1]

    def right(q, pair):
        at = pl.ds(pl.multiple_of(pair * (2 * n_col), 2 * n_col), 2 * n_col)
        return dot3(st_hi[at, :], st_lo[at, :], l2_hi[q], l2_lo[q], NN)

    def copy_a(q):
        return remote(tmp_a.at[q, 1 - core], recv_a.at[q], a_s.at[q], a_r.at[q], "tins", mate)

    def copy_y(q):
        return remote(sum_a.at[q], recv_y.at[q], y_s.at[q], y_r.at[q], "tins", far)

    def copy_b(q):
        return remote(tmp_b.at[q, 1 - core], recv_b.at[q], b_s.at[q], b_r.at[q], "tins", mate)

    def relay(q):
        copy_a(q).wait_recv()
        sum_a[q] = tmp_a[q, core] + recv_a[q]
        copy_y(q).start()

    my_pair = me_t // 2

    def near(q):
        res = right(q, 1 - my_pair)
        tmp_a[q, 0] = res[:n_col]
        tmp_a[q, 1] = res[n_col:]
        copy_a(q).start()

    for g in range(n_group + 2):
        if g < n_group:
            reduce(g)
        if 1 <= g <= n_group:
            forward(g - 1)
        if g >= 2:
            left(g - 2)
            for q in range((g - 2) * per_group, (g - 1) * per_group):
                near(q)
                if q:
                    relay(q - 1)
    relay(pairs - 1)
    for q in range(pairs):
        res = right(q, my_pair)
        tmp_b[q, 0] = res[:n_col]
        tmp_b[q, 1] = res[n_col:]
        copy_b(q).start()
    for q in range(pairs):
        copy_b(q).wait_recv()
        copy_y(q).wait_recv()
        val = tmp_b[q, core] + recv_b[q] + recv_y[q]
        for part in range(2):
            out_ref[pl.ds(2 * q + part, n_col, stride=pairs2), :] = (
                val[:, part * rows:(part + 1) * rows])

    for z in order:
        for copy in bra_copies[z]:
            copy.wait_send()
    for g in range(n_group):
        for d in range(1, n_sp):
            rs_copy(g, d).wait_send()
            ag_copy(g, d).wait_send()
        for slot in range(n_sp):
            for d in range(1, n_ts):
                fx_copy(g, slot, d).wait_send()
    for q in range(pairs):
        copy_a(q).wait_send()
        copy_y(q).wait_send()
        copy_b(q).wait_send()


def pair_kernel(
    n_sp, dir_ref, mom_ref, ins_ref, sink_ref, ev_ref, link_ref, p_ref, s_ref, out_ref,
    cos_ref, sin_ref, p_vm, s_vm, in_sem,
    vec_own, vec_far, w_top, halo_up, halo_dn, ket_hi, ket_lo, rhs_own, rhs_far, acc_own, acc_far,
    part_own, part_far, buf_own, buf_far, sum_own, sum_far, e_full, e_hi, e_lo, st_hi, st_lo,
    p2_hi, p2_lo, l2_hi, l2_lo, tmp_a, recv_a, sum_a, tmp_b, recv_b, recv_y,
    loc_sem, v_s, v_r, halo_s, halo_r, rd_s, rd_r, gd_s, gd_r, xd_s, xd_r,
    rf_s, rf_r, gf_s, gf_r, xf_s, xf_r, a_s, a_r, y_s, y_r, b_s, b_r,
):
    _, vecs, depth, plane = ev_ref.shape
    pairs = part_own.shape[1]
    n_dir = 3
    n_mom = pairs // n_dir
    nv = 2 * vecs
    me_x = lax.axis_index("tsink")
    me_z = lax.axis_index("space")
    me_t = lax.axis_index("tins")
    core = me_t % 2
    mate = me_t + 1 - 2 * core
    far = (me_t + 2) % 4
    up = (me_z + 1) % n_sp
    down = (me_z + n_sp - 1) % n_sp
    other = 1 - me_x
    is_head = me_x == core
    not_head = me_x != core

    local = [
        pltpu.make_async_copy(ev_ref.at[:, :, z, :], vec_own.at[z], loc_sem.at[z])
        for z in range(depth)
    ]
    for copy in reversed(local):
        copy.start()
    load_p = pltpu.make_async_copy(p_ref, p_vm, in_sem.at[0])
    load_s = pltpu.make_async_copy(s_ref, s_vm, in_sem.at[1])
    load_p.start()
    load_s.start()
    barrier = pltpu.get_barrier_semaphore()
    mesh_type = pl.DeviceIdType.MESH
    pl.semaphore_signal(barrier, inc=1, device_id={"tsink": other}, device_id_type=mesh_type)
    for d in range(1, n_sp):
        pl.semaphore_signal(barrier, inc=1, device_id={"space": (me_z + d) % n_sp},
                            device_id_type=mesh_type)
    for target in (mate, far):
        pl.semaphore_signal(barrier, inc=1, device_id={"tins": target}, device_id_type=mesh_type)
    pl.semaphore_wait(barrier, 1 + n_sp - 1 + 2)

    order = list(range(1, depth - 1)) + [0, depth - 1]
    vec_copies = {
        z: remote(ev_ref.at[:, :, z, :], vec_far.at[z], v_s.at[z], v_r.at[z], "tsink", other)
        for z in order
    }
    halo_v = remote(ev_ref.at[:, :, 0, :], halo_up, halo_s.at[0], halo_r.at[0], "space", down)
    halo_w = remote(w_top, halo_dn, halo_s.at[1], halo_r.at[1], "space", up)

    @pl.when(is_head)
    def _():
        halo_v.start()

    @pl.when(not_head)
    def _():
        for z in order:
            vec_copies[z].start()

    block = min(16, vecs)
    n_block = vecs // block

    def rows_of(b):
        return pl.ds(pl.multiple_of(b * block, block), block)

    def own(z, c, b):
        return vec_own[z, c, rows_of(b), :]

    def links_at(k, z):
        return [
            [[link_ref[k, part, i, j, pl.ds(z, 1), :] for j in range(3)] for i in range(3)]
            for part in range(2)
        ]

    column = lax.broadcasted_iota(jnp.int32, (block, plane), 1) % L

    def shifted(x, k, sign):
        if k == 1:
            return pltpu.roll(x, plane - L if sign > 0 else L, axis=1)
        if sign > 0:
            return jnp.where(column == L - 1, pltpu.roll(x, L - 1, axis=1),
                             pltpu.roll(x, plane - 1, axis=1))
        return jnp.where(column == 0, pltpu.roll(x, plane + 1 - L, axis=1),
                         pltpu.roll(x, 1, axis=1))

    site = lax.broadcasted_iota(jnp.int32, (depth, plane), 1)
    z_coord = me_z * depth + lax.broadcasted_iota(jnp.int32, (depth, plane), 0)
    for m in range(n_mom):
        product = mom_ref[m, 0] * (site % L) + mom_ref[m, 1] * (site // L) + mom_ref[m, 2] * z_coord
        steps = [0] + [mom_ref[m, k] for k in range(n_dir)] + [-mom_ref[m, k] for k in range(n_dir)]
        for j, step in enumerate(steps):
            angles = (2.0 * math.pi / L) * jnp.bitwise_and(product + step, L - 1).astype(F32)
            cos_ref[m, j] = jnp.cos(angles)
            sin_ref[m, j] = jnp.sin(angles)

    def put_kets(k, z, b, ahead, back):
        deriv = [ahead[c] - back[c] for c in range(6)]

        def put(start, i, re, im):
            at = pl.multiple_of(start * vecs + b * block, block)
            for comp, val in ((i, re), (3 + i, im)):
                hi, lo = split(val)
                cols = slice(comp * plane, (comp + 1) * plane)
                ket_hi[z, pl.ds(at, block), cols] = hi
                ket_lo[z, pl.ds(at, block), cols] = lo

        for m in range(n_mom):
            c, c_up, c_dn = [cos_ref[m, j, pl.ds(z, 1), :] for j in (0, 1 + k, 1 + n_dir + k)]
            s, s_up, s_dn = [sin_ref[m, j, pl.ds(z, 1), :] for j in (0, 1 + k, 1 + n_dir + k)]
            for i in range(3):
                put(m * n_dir + k, i, c * deriv[i] + s * deriv[3 + i],
                    c * deriv[3 + i] - s * deriv[i])
                put(pairs + m * n_dir + k, i,
                    c_up * ahead[i] - s_up * ahead[3 + i] - c_dn * back[i] + s_dn * back[3 + i],
                    c_up * ahead[3 + i] + s_up * ahead[i] - c_dn * back[3 + i] - s_dn * back[i])

    local[depth - 1].wait()

    def top_body(b, carry):
        vec = [own(depth - 1, c, b) for c in range(6)]
        w = colour_rows(links_at(2, depth - 1), vec, True)
        for c in range(6):
            w_top[c, rows_of(b), :] = w[c]
        return carry

    lax.fori_loop(0, n_block, top_body, 0)

    @pl.when(is_head)
    def _():
        halo_w.start()

    for copy in local[:-1]:
        copy.wait()

    for k in range(2):
        def xy_body(t, carry, k=k):
            z = t // n_block
            b = t % n_block
            vec = [own(z, c, b) for c in range(6)]
            link = links_at(k, z)
            ahead = colour_rows(link, [shifted(x, k, 1) for x in vec], False)
            back = colour_rows(link, vec, True)
            put_kets(k, z, b, ahead, [shifted(x, k, -1) for x in back])
            return carry

        lax.fori_loop(0, depth * n_block, xy_body, 0)

    @pl.when(not_head)
    def _():
        halo_v.start()
        halo_w.start()

    def z_planes(z, b, above, below):
        put_kets(2, z, b, colour_rows(links_at(2, z), above, False), below)

    def own_back(z, b):
        return colour_rows(links_at(2, z), [own(z, c, b) for c in range(6)], True)

    def mid_body(t, carry):
        z = t // n_block + 1
        b = t % n_block
        z_planes(z, b, [own(z + 1, c, b) for c in range(6)], own_back(z - 1, b))
        return carry

    lax.fori_loop(0, (depth - 2) * n_block, mid_body, 0)

    def fill(rhs, vec, z):
        for c in range(3):
            left_cols = slice(c * plane, (c + 1) * plane)
            right_cols = slice((3 + c) * plane, (4 + c) * plane)
            for at, re, im in zip((0, nv), split(vec[z, c]), split(vec[z, 3 + c])):
                rhs[at:at + vecs, left_cols] = re
                rhs[at:at + vecs, right_cols] = im
                rhs[at + vecs:at + nv, left_cols] = -im
                rhs[at + vecs:at + nv, right_cols] = re

    def elemental(z, rhs, acc, start):
        rows = pairs * vecs
        both = lax.dot_general(ket_hi[z, start:start + rows, :], rhs[...], NT,
                               preferred_element_type=F32)
        low = lax.dot_general(ket_lo[z, start:start + rows, :], rhs[0:nv, :], NT,
                              preferred_element_type=F32)
        part = (both[:, :nv] + both[:, nv:] + low).reshape(pairs, vecs, nv)
        at = slice(start // vecs, start // vecs + pairs)
        if z == order[0]:
            acc[at] = part
        else:
            acc[at] += part

    def own_elemental(z):
        fill(rhs_own, vec_own, z)
        elemental(z, rhs_own, acc_own, 0)

    def far_elemental(z):
        @pl.when(is_head)
        def _():
            vec_copies[z].wait_recv()
            fill(rhs_far, vec_far, z)
            for start in (0, pairs * vecs):
                elemental(z, rhs_far, acc_far, start)

    for z in order[:-2]:
        own_elemental(z)

    load_s.wait()
    load_p.wait()
    half = s_ref.shape[1]
    for part in range(2):
        def st_body(cb, carry, part=part):
            c_at = pl.multiple_of(cb * 128, 128)
            for kb in range(half // nv):
                near_at = pl.multiple_of(kb * nv + core * vecs, vecs)
                far_at = pl.multiple_of(kb * nv + (1 - core) * vecs, vecs)
                tile = jnp.concatenate([s_vm[part, pl.ds(near_at, vecs), pl.ds(c_at, 128)],
                                        s_vm[part, pl.ds(far_at, vecs), pl.ds(c_at, 128)]], axis=0).T
                hi, lo = split(tile)
                cols = slice(part * half + kb * nv, part * half + (kb + 1) * nv)
                st_hi[pl.ds(c_at, 128), cols] = hi
                st_lo[pl.ds(c_at, 128), cols] = lo
            return carry

        lax.fori_loop(0, half // 128, st_body, 0)
    weight = jnp.where(ins_ref[0] < sink_ref[0], 1.0, 0.0).astype(F32)
    rows = p_ref.shape[1]
    low_lane = lax.broadcasted_iota(jnp.int32, (rows, nv), 1) < vecs
    for spin in range(NSPIN):
        scale = weight if spin < 2 else -weight
        re = p_vm[0, :, spin * nv:(spin + 1) * nv] * scale
        im = p_vm[1, :, spin * nv:(spin + 1) * nv] * scale
        re_roll = pltpu.roll(re, vecs, axis=1)
        im_roll = pltpu.roll(im, vecs, axis=1)
        re, re_roll = jnp.where(core == 0, re, re_roll), jnp.where(core == 0, re_roll, re)
        im, im_roll = jnp.where(core == 0, im, im_roll), jnp.where(core == 0, im_roll, im)
        for row, (x, x_roll, y, y_roll) in enumerate(((re, re_roll, -im, -im_roll),
                                                      (im, im_roll, re, re_roll))):
            for col, val in enumerate((jnp.where(low_lane, x, y_roll), jnp.where(low_lane, x_roll, y))):
                hi, lo = split(val)
                p2_hi[spin, row * rows:(row + 1) * rows, col * nv:(col + 1) * nv] = hi
                p2_lo[spin, row * rows:(row + 1) * rows, col * nv:(col + 1) * nv] = lo

    halo_w.wait()

    def low_body(b, carry):
        above = [own(1, c, b) for c in range(6)]
        z_planes(0, b, above, [halo_dn[c, rows_of(b), :] for c in range(6)])
        return carry

    lax.fori_loop(0, n_block, low_body, 0)
    halo_v.wait()

    def high_body(b, carry):
        above = [halo_up[c, rows_of(b), :] for c in range(6)]
        z_planes(depth - 1, b, above, own_back(depth - 2, b))
        return carry

    lax.fori_loop(0, n_block, high_body, 0)
    for z in order[-2:]:
        own_elemental(z)

    strip = vecs // n_sp
    per_group = part_far.shape[2]
    n_group = pairs // per_group
    my_strip = pl.ds(pl.multiple_of(me_z * strip, strip), strip)
    corner = jnp.where(is_head, 0, 3)

    def chosen(acc, q, base):
        return acc[base + (q // n_dir) * n_dir + dir_ref[q % n_dir]]

    def strips(val):
        return [val[z * strip:(z + 1) * strip, :] for z in range(n_sp)]

    for q in range(pairs):
        for z, val in enumerate(strips(chosen(acc_own, q, 0))):
            part_own[z, q] = val

    def rd_copy(d):
        peer = (me_z + d) % n_sp
        return remote(part_own.at[peer], buf_own.at[d - 1], rd_s.at[d - 1], rd_r.at[d - 1],
                      "space", peer)

    def gd_copy(d):
        return remote(sum_own, e_full.at[:, corner, my_strip, :], gd_s.at[d - 1], gd_r.at[d - 1],
                      "space", (me_z + d) % n_sp)

    def xd_copy(g):
        block_at = e_full.at[pl.ds(g * per_group, per_group), corner]
        return remote(block_at, block_at, xd_s.at[g], xd_r.at[g], "tsink", other)

    def rf_copy(g, d):
        peer = (me_z + d) % n_sp
        return remote(part_far.at[g, peer], buf_far.at[g, d - 1], rf_s.at[g, d - 1],
                      rf_r.at[g, d - 1], "space", peer)

    def mixed(g, strip_at):
        return e_full.at[pl.ds(g * per_group, per_group), pl.ds(1, 2), strip_at, :]

    def gf_copy(g, d):
        return remote(sum_far.at[g], mixed(g, my_strip), gf_s.at[g, d - 1], gf_r.at[g, d - 1],
                      "space", (me_z + d) % n_sp)

    def xf_copy(g, slot):
        owner = (me_z + n_sp - slot) % n_sp
        target = mixed(g, pl.ds(pl.multiple_of(owner * strip, strip), strip))
        return remote(target if slot else sum_far.at[g], target, xf_s.at[g, slot], xf_r.at[g, slot],
                      "tsink", other)

    for d in range(1, n_sp):
        rd_copy(d).start()
    for z in order[:-1]:
        far_elemental(z)
    total = part_own[me_z]
    for d in range(1, n_sp):
        rd_copy(d).wait_recv()
        total = total + buf_own[d - 1]
    sum_own[...] = total
    e_full[:, corner, my_strip, :] = total
    for d in range(1, n_sp):
        gd_copy(d).start()
    far_elemental(order[-1])

    @pl.when(is_head)
    def _():
        for q in range(pairs):
            g, i = q // per_group, q % per_group
            for z, val in enumerate(strips(chosen(acc_far, q, 0))):
                part_far[g, z, i, 0] = val
            turned = chosen(acc_far, q, pairs).T
            turned = jnp.concatenate([-turned[:vecs], turned[vecs:]], axis=1)
            for z, val in enumerate(strips(turned)):
                part_far[g, z, i, 1] = val
            if i == per_group - 1:
                for d in range(1, n_sp):
                    rf_copy(g, d).start()

    @pl.when(not_head)
    def _():
        for z in order:
            vec_copies[z].wait_send()

    for d in range(1, n_sp):
        gd_copy(d).wait_recv()

    def reduce(g):
        @pl.when(is_head)
        def _():
            total = part_far[g, me_z]
            for d in range(1, n_sp):
                rf_copy(g, d).wait_recv()
                total = total + buf_far[g, d - 1]
            sum_far[g] = total
            e_full[pl.ds(g * per_group, per_group), pl.ds(1, 2), my_strip, :] = total
            for d in range(1, n_sp):
                gf_copy(g, d).start()
            xf_copy(g, 0).start()

    def forward(g):
        @pl.when(is_head)
        def _():
            for slot in range(1, n_sp):
                gf_copy(g, slot).wait_recv()
                xf_copy(g, slot).start()

    def left(g):
        xd_copy(g).wait_recv()

        @pl.when(not_head)
        def _():
            for slot in range(n_sp):
                xf_copy(g, slot).wait_recv()

        for i in range(per_group):
            for quad in range(4):
                hi, lo = split(e_full[g * per_group + i, quad])
                at = i * nv + quad // 2 * vecs
                cols = slice(quad % 2 * nv, (quad % 2 + 1) * nv)
                e_hi[at:at + vecs, cols] = hi
                e_lo[at:at + vecs, cols] = lo

        def left_body(spin, carry):
            prod = dot3(e_hi[...], e_lo[...], p2_hi[spin], p2_lo[spin], NT)
            at = pl.ds(pl.multiple_of(spin * nv, nv), nv)
            at_low = pl.ds(pl.multiple_of(half + spin * nv, nv), nv)
            for i in range(per_group):
                hi, lo = split(prod[i * nv:(i + 1) * nv])
                for ref, val in ((l2_hi, hi), (l2_lo, lo)):
                    ref[g * per_group + i, at, :] = val
                    ref[g * per_group + i, at_low, 0:rows] = -val[:, rows:]
                    ref[g * per_group + i, at_low, rows:] = val[:, :rows]
            return carry

        lax.fori_loop(0, NSPIN, left_body, 0)

    n_col = recv_a.shape[1]

    def right(q, pair):
        at = pl.ds(pl.multiple_of(pair * (2 * n_col), 2 * n_col), 2 * n_col)
        return dot3(st_hi[at, :], st_lo[at, :], l2_hi[q], l2_lo[q], NN)

    def copy_a(q):
        return remote(tmp_a.at[q, 1 - core], recv_a.at[q], a_s.at[q], a_r.at[q], "tins", mate)

    def copy_y(q):
        return remote(sum_a.at[q], recv_y.at[q], y_s.at[q], y_r.at[q], "tins", far)

    def copy_b(q):
        return remote(tmp_b.at[q, 1 - core], recv_b.at[q], b_s.at[q], b_r.at[q], "tins", mate)

    def relay(q):
        copy_a(q).wait_recv()
        sum_a[q] = tmp_a[q, core] + recv_a[q]
        copy_y(q).start()

    my_pair = me_t // 2

    def near(q):
        res = right(q, 1 - my_pair)
        tmp_a[q, 0] = res[:n_col]
        tmp_a[q, 1] = res[n_col:]
        copy_a(q).start()

    for g in range(n_group + 2):
        if g < n_group:
            xd_copy(g).start()
            reduce(g)
        if 1 <= g <= n_group:
            forward(g - 1)
        if g >= 2:
            left(g - 2)
            for q in range((g - 2) * per_group, (g - 1) * per_group):
                near(q)
                if q:
                    relay(q - 1)
    relay(pairs - 1)
    for q in range(pairs):
        res = right(q, my_pair)
        tmp_b[q, 0] = res[:n_col]
        tmp_b[q, 1] = res[n_col:]
        copy_b(q).start()
    for q in range(pairs):
        copy_b(q).wait_recv()
        copy_y(q).wait_recv()
        val = tmp_b[q, core] + recv_b[q] + recv_y[q]
        for part in range(2):
            out_ref[pl.ds(2 * q + part, n_col, stride=2 * pairs), :] = (
                val[:, part * rows:(part + 1) * rows])

    for d in range(1, n_sp):
        rd_copy(d).wait_send()
        gd_copy(d).wait_send()

    @pl.when(is_head)
    def _():
        for g in range(n_group):
            for d in range(1, n_sp):
                rf_copy(g, d).wait_send()
                gf_copy(g, d).wait_send()
            for slot in range(n_sp):
                xf_copy(g, slot).wait_send()

    for g in range(n_group):
        xd_copy(g).wait_send()
    for q in range(pairs):
        copy_a(q).wait_send()
        copy_y(q).wait_send()
        copy_b(q).wait_send()


def copy_kernel(in_ref, out_ref):
    out_ref[...] = in_ref[...]


def ring_call(n_ts, n_sp, n_ti, eigvecs, links, momenta, directions, ins_time, sink_time,
              sink_peramb, source_peramb):
    assert n_ti == 4
    _, _, _, vecs, depth, plane = eigvecs.shape
    nv = vecs * n_ts
    ev = eigvecs.reshape(6, vecs, depth, plane)
    pairs = momenta.shape[0] * directions.shape[0]
    order_m = source_peramb.shape[-1]
    rows = sink_peramb.shape[3]
    n_col = order_m // n_ti
    n_group = 2 * pairs // n_sp
    v = pltpu.VMEM
    dma = pltpu.SemaphoreType.DMA
    scratch = [
        v((momenta.shape[0], depth, plane), F32), v((momenta.shape[0], depth, plane), F32),
        v(sink_peramb.shape[2:], F32), v(source_peramb.shape[1:], F32), dma((2,)),
        v((depth, 6, nv, plane), F32),
        v((6, vecs, plane), F32), v((6, vecs, plane), F32), v((6, vecs, plane), F32),
        v((depth, pairs * vecs, 6 * plane), BF16), v((depth, pairs * vecs, 6 * plane), BF16),
        v((2 * nv, 6 * plane), BF16), v((2 * nv, 6 * plane), BF16),
        v((pairs, vecs, 2 * nv), F32),
        v((2 * pairs, vecs, nv), F32),
        v((n_group, n_sp - 1, vecs, nv), F32),
        v((n_group, vecs, nv), F32),
        v((2 * pairs, nv, nv), F32),
        v((n_sp // 2 * nv, 2 * nv), BF16), v((n_sp // 2 * nv, 2 * nv), BF16),
        v((order_m, 2 * order_m), BF16), v((order_m, 2 * order_m), BF16),
        v((NSPIN, 2 * rows, 2 * nv), BF16), v((NSPIN, 2 * rows, 2 * nv), BF16),
        v((pairs, 2 * order_m, 2 * rows), BF16), v((pairs, 2 * order_m, 2 * rows), BF16),
        v((pairs, 2, n_col, 2 * rows), F32),
        v((pairs, n_col, 2 * rows), F32), v((pairs, n_col, 2 * rows), F32),
        v((pairs, 2, n_col, 2 * rows), F32),
        v((pairs, n_col, 2 * rows), F32), v((pairs, n_col, 2 * rows), F32),
        dma((depth,)), dma((depth, n_ts - 1)), dma((depth, n_ts - 1)), dma((2,)), dma((2,)),
        dma((n_group, n_sp - 1)), dma((n_group, n_sp - 1)),
        dma((n_group, n_sp - 1)), dma((n_group, n_sp - 1)),
        dma((n_group, n_sp, n_ts - 1)), dma((n_group, n_sp, n_ts - 1)),
        dma((pairs,)), dma((pairs,)), dma((pairs,)), dma((pairs,)), dma((pairs,)), dma((pairs,)),
    ]
    smem = pl.BlockSpec(memory_space=pltpu.SMEM)
    vmem = pl.BlockSpec(memory_space=pltpu.VMEM)
    hbm = pl.BlockSpec(memory_space=pl.ANY)
    out = pl.pallas_call(
        functools.partial(ring_kernel, n_ts, n_sp),
        out_shape=jax.ShapeDtypeStruct((n_col * pairs * 2, rows), F32),
        in_specs=[smem] * 4 + [hbm, vmem, hbm, hbm],
        out_specs=vmem,
        scratch_shapes=scratch,
        compiler_params=pltpu.CompilerParams(
            collective_id=0, has_side_effects=True, vmem_limit_bytes=60 * 1024 * 1024
        ),
        name="peramb",
    )(directions, momenta, ins_time, sink_time, ev, links[0], sink_peramb[0, 0],
      source_peramb[0])
    tile = pl.BlockSpec((out.shape[0] // 2, rows), lambda i: (i, 0))
    out = pl.pallas_call(
        copy_kernel,
        grid=(2,),
        out_shape=jax.ShapeDtypeStruct(out.shape, F32),
        in_specs=[tile],
        out_specs=tile,
        name="result",
    )(out)
    return out.reshape(n_col, 1, pairs, 2, rows)


def pair_call(n_ts, n_sp, n_ti, eigvecs, links, momenta, directions, ins_time, sink_time,
              sink_peramb, source_peramb):
    assert n_ts == 2 and n_ti == 4
    _, _, _, vecs, depth, plane = eigvecs.shape
    nv = vecs * n_ts
    ev = eigvecs.reshape(6, vecs, depth, plane)
    n_mom = momenta.shape[0]
    pairs = n_mom * directions.shape[0]
    order_m = source_peramb.shape[-1]
    rows = sink_peramb.shape[3]
    n_col = order_m // n_ti
    per_group = 2
    n_group = pairs // per_group
    strip = vecs // n_sp
    v = pltpu.VMEM
    dma = pltpu.SemaphoreType.DMA
    scratch = [
        v((n_mom, 7, depth, plane), F32), v((n_mom, 7, depth, plane), F32),
        v(sink_peramb.shape[2:], F32), v(source_peramb.shape[1:], F32), dma((2,)),
        v((depth, 6, vecs, plane), F32), v((depth, 6, vecs, plane), F32),
        v((6, vecs, plane), F32), v((6, vecs, plane), F32), v((6, vecs, plane), F32),
        v((depth, 2 * pairs * vecs, 6 * plane), BF16), v((depth, 2 * pairs * vecs, 6 * plane), BF16),
        v((2 * nv, 6 * plane), BF16), v((2 * nv, 6 * plane), BF16),
        v((pairs, vecs, nv), F32), v((2 * pairs, vecs, nv), F32),
        v((n_sp, pairs, strip, nv), F32), v((n_group, n_sp, per_group, 2, strip, nv), F32),
        v((n_sp - 1, pairs, strip, nv), F32), v((n_group, n_sp - 1, per_group, 2, strip, nv), F32),
        v((pairs, strip, nv), F32), v((n_group, per_group, 2, strip, nv), F32),
        v((pairs, 4, vecs, nv), F32),
        v((per_group * nv, 2 * nv), BF16), v((per_group * nv, 2 * nv), BF16),
        v((order_m, 2 * order_m), BF16), v((order_m, 2 * order_m), BF16),
        v((NSPIN, 2 * rows, 2 * nv), BF16), v((NSPIN, 2 * rows, 2 * nv), BF16),
        v((pairs, 2 * order_m, 2 * rows), BF16), v((pairs, 2 * order_m, 2 * rows), BF16),
        v((pairs, 2, n_col, 2 * rows), F32),
        v((pairs, n_col, 2 * rows), F32), v((pairs, n_col, 2 * rows), F32),
        v((pairs, 2, n_col, 2 * rows), F32),
        v((pairs, n_col, 2 * rows), F32), v((pairs, n_col, 2 * rows), F32),
        dma((depth,)), dma((depth,)), dma((depth,)), dma((2,)), dma((2,)),
        dma((n_sp - 1,)), dma((n_sp - 1,)), dma((n_sp - 1,)), dma((n_sp - 1,)),
        dma((n_group,)), dma((n_group,)),
        dma((n_group, n_sp - 1)), dma((n_group, n_sp - 1)),
        dma((n_group, n_sp - 1)), dma((n_group, n_sp - 1)),
        dma((n_group, n_sp)), dma((n_group, n_sp)),
        dma((pairs,)), dma((pairs,)), dma((pairs,)), dma((pairs,)), dma((pairs,)), dma((pairs,)),
    ]
    smem = pl.BlockSpec(memory_space=pltpu.SMEM)
    vmem = pl.BlockSpec(memory_space=pltpu.VMEM)
    hbm = pl.BlockSpec(memory_space=pl.ANY)
    out = pl.pallas_call(
        functools.partial(pair_kernel, n_sp),
        out_shape=jax.ShapeDtypeStruct((n_col * pairs * 2, rows), F32),
        in_specs=[smem] * 4 + [hbm, vmem, hbm, hbm],
        out_specs=vmem,
        scratch_shapes=scratch,
        compiler_params=pltpu.CompilerParams(
            collective_id=0, has_side_effects=True, vmem_limit_bytes=60 * 1024 * 1024
        ),
        name="peramb",
    )(directions, momenta, ins_time, sink_time, ev, links[0], sink_peramb[0, 0],
      source_peramb[0])
    tile = pl.BlockSpec((out.shape[0] // 2, rows), lambda i: (i, 0))
    out = pl.pallas_call(
        copy_kernel,
        grid=(2,),
        out_shape=jax.ShapeDtypeStruct(out.shape, F32),
        in_specs=[tile],
        out_specs=tile,
        name="result",
    )(out)
    return out.reshape(n_col, 1, pairs, 2, rows)


def solution(mesh):
    in_specs = (
        P("tins", None, None, "tsink", "space", None),
        P("tins", None, None, None, None, "space", None),
        P(),
        P(),
        P("tins"),
        P("tsink"),
        P("tsink", "tins", None, "space", None),
        P("tins", None, None, None),
    )
    out_specs = P("tins", "tsink", None, None, "space")
    sizes = mesh.shape["tsink"], mesh.shape["space"], mesh.shape["tins"]
    body = functools.partial(pair_call if sizes[0] == 2 else ring_call, *sizes)
    return jax.shard_map(body, mesh=mesh, in_specs=in_specs, out_specs=out_specs, check_vma=False)
```

```python
import functools
import math

import jax
import jax.numpy as jnp
from jax import lax
from jax.experimental import pallas as pl
from jax.experimental.pallas import tpu as pltpu
from jax.sharding import PartitionSpec as P

L = 16
NSPIN = 4
BF16 = jnp.bfloat16
F32 = jnp.float32
NT = (((1,), (1,)), ((), ()))
NN = (((1,), (0,)), ((), ()))


def split(x):
    hi = x.astype(BF16)
    return hi, (x - hi.astype(F32)).astype(BF16)


def dot3(a_hi, a_lo, b_hi, b_lo, dims):
    def one(a, b):
        return lax.dot_general(a, b, dims, preferred_element_type=F32)

    return one(a_hi, b_hi) + one(a_hi, b_lo) + one(a_lo, b_hi)


def dot_two(a, b_hi, b_lo, dims):
    rows = a.shape[0] // 2
    both = lax.dot_general(a, b_hi, dims, preferred_element_type=F32)
    low = lax.dot_general(a[:rows], b_lo, dims, preferred_element_type=F32)
    return both[:rows] + both[rows:] + low


def remote(src, dst, send, recv, axis, index):
    return pltpu.make_async_remote_copy(
        src_ref=src,
        dst_ref=dst,
        send_sem=send,
        recv_sem=recv,
        device_id={axis: index},
        device_id_type=pl.DeviceIdType.MESH,
    )


def colour_rows(link, vec, adjoint):
    rows = []
    for i in range(3):
        re = im = None
        for j in range(3):
            if adjoint:
                a, b = link[0][j][i], link[1][j][i]
                tr = a * vec[j] + b * vec[3 + j]
                ti = a * vec[3 + j] - b * vec[j]
            else:
                a, b = link[0][i][j], link[1][i][j]
                tr = a * vec[j] - b * vec[3 + j]
                ti = a * vec[3 + j] + b * vec[j]
            re = tr if re is None else re + tr
            im = ti if im is None else im + ti
        rows.append((re, im))
    return [r[0] for r in rows] + [r[1] for r in rows]


def ring_kernel(
    n_ts, n_sp, dir_ref, mom_ref, ins_ref, sink_ref, ev_ref, link_ref, p_ref, s_ref, out_ref,
    cos_ref, sin_ref, p_vm, s_vm, in_sem,
    bra, w_top, halo_up, halo_dn, ket_hi, ket_lo, rhs_hi, rhs_lo, acc, epart, rs_buf, e_own,
    e_full, e_hi, e_lo, st_hi, st_lo, p2_hi, p2_lo, l2_hi, l2_lo, tmp_a, recv_a, sum_a, tmp_b,
    recv_b, recv_y, loc_sem, bra_s, bra_r, halo_s, halo_r, rs_s, rs_r, ag_s, ag_r, fx_s, fx_r,
    a_s, a_r, y_s, y_r, b_s, b_r,
):
    _, vecs, depth, plane = ev_ref.shape
    pairs2 = epart.shape[0]
    pairs = pairs2 // 2
    n_dir = 3
    n_mom = pairs // n_dir
    nv = bra.shape[2]
    me_x = lax.axis_index("tsink")
    me_z = lax.axis_index("space")
    me_t = lax.axis_index("tins")
    core = me_t % 2
    mate = me_t + 1 - 2 * core
    far = (me_t + 2) % 4
    up = (me_z + 1) % n_sp
    down = (me_z + n_sp - 1) % n_sp
    my_rows = pl.ds(pl.multiple_of(me_x * vecs, vecs), vecs)
    local = [
        pltpu.make_async_copy(ev_ref.at[:, :, z, :], bra.at[z, :, my_rows, :], loc_sem.at[z])
        for z in range(depth)
    ]
    for copy in reversed(local):
        copy.start()
    load_p = pltpu.make_async_copy(p_ref, p_vm, in_sem.at[0])
    load_s = pltpu.make_async_copy(s_ref, s_vm, in_sem.at[1])
    load_p.start()
    load_s.start()
    barrier = pltpu.get_barrier_semaphore()
    mesh_type = pl.DeviceIdType.MESH
    for d in range(1, n_ts):
        pl.semaphore_signal(barrier, inc=1, device_id={"tsink": (me_x + d) % n_ts},
                            device_id_type=mesh_type)
    for d in range(1, n_sp):
        pl.semaphore_signal(barrier, inc=1, device_id={"space": (me_z + d) % n_sp},
                            device_id_type=mesh_type)
    for target in (mate, far):
        pl.semaphore_signal(barrier, inc=1, device_id={"tins": target}, device_id_type=mesh_type)
    pl.semaphore_wait(barrier, n_ts - 1 + n_sp - 1 + 2)

    order = list(range(1, depth - 1)) + [0, depth - 1]
    bra_copies = {}
    for z in order:
        bra_copies[z] = [
            remote(ev_ref.at[:, :, z, :], bra.at[z, :, my_rows, :], bra_s.at[z, d - 1], bra_r.at[z, d - 1],
                   "tsink", (me_x + d) % n_ts)
            for d in range(1, n_ts)
        ]
    halo_v = remote(ev_ref.at[:, :, 0, :], halo_up, halo_s.at[0], halo_r.at[0], "space", down)
    halo_w = remote(w_top, halo_dn, halo_s.at[1], halo_r.at[1], "space", up)
    halo_v.start()
    for z in order:
        for copy in bra_copies[z]:
            copy.start()

    block = min(16, vecs)
    n_block = vecs // block

    def rows_of(b):
        return pl.ds(pl.multiple_of(b * block, block), block)

    def own(z, c, b):
        return bra[z, c, pl.ds(pl.multiple_of(me_x * vecs + b * block, block), block), :]

    def links_at(k, z):
        return [
            [[link_ref[k, part, i, j, pl.ds(z, 1), :] for j in range(3)] for i in range(3)]
            for part in range(2)
        ]

    column = lax.broadcasted_iota(jnp.int32, (block, plane), 1) % L

    def shifted(x, k, sign):
        if k == 1:
            return pltpu.roll(x, plane - L if sign > 0 else L, axis=1)
        if sign > 0:
            return jnp.where(column == L - 1, pltpu.roll(x, L - 1, axis=1),
                             pltpu.roll(x, plane - 1, axis=1))
        return jnp.where(column == 0, pltpu.roll(x, plane + 1 - L, axis=1),
                         pltpu.roll(x, 1, axis=1))

    site = lax.broadcasted_iota(jnp.int32, (depth, plane), 1)
    z_coord = me_z * depth + lax.broadcasted_iota(jnp.int32, (depth, plane), 0)
    for m in range(n_mom):
        product = mom_ref[m, 0] * (site % L) + mom_ref[m, 1] * (site // L) + mom_ref[m, 2] * z_coord
        angles = (2.0 * math.pi / L) * jnp.bitwise_and(product, L - 1).astype(F32)
        cos_ref[m] = jnp.cos(angles)
        sin_ref[m] = jnp.sin(angles)

    def put_kets(k, z, b, deriv):
        for m in range(n_mom):
            c = cos_ref[m, pl.ds(z, 1), :]
            s = sin_ref[m, pl.ds(z, 1), :]
            start = pl.multiple_of((m * n_dir + k) * vecs + b * block, block)
            for i in range(3):
                for comp, val in (
                    (i, c * deriv[i] + s * deriv[3 + i]),
                    (3 + i, c * deriv[3 + i] - s * deriv[i]),
                ):
                    hi, lo = split(val)
                    cols = slice(comp * plane, (comp + 1) * plane)
                    ket_hi[z, pl.ds(start, block), cols] = hi
                    ket_lo[z, pl.ds(start, block), cols] = lo

    local[depth - 1].wait()

    def top_body(b, carry):
        vec = [own(depth - 1, c, b) for c in range(6)]
        w = colour_rows(links_at(2, depth - 1), vec, True)
        for c in range(6):
            w_top[c, rows_of(b), :] = w[c]
        return carry

    lax.fori_loop(0, n_block, top_body, 0)
    halo_w.start()
    for copy in local[:-1]:
        copy.wait()

    for k in range(2):
        def xy_body(t, carry, k=k):
            z = t // n_block
            b = t % n_block
            vec = [own(z, c, b) for c in range(6)]
            link = links_at(k, z)
            ahead = colour_rows(link, [shifted(x, k, 1) for x in vec], False)
            back = colour_rows(link, vec, True)
            put_kets(k, z, b, [ahead[c] - shifted(back[c], k, -1) for c in range(6)])
            return carry

        lax.fori_loop(0, depth * n_block, xy_body, 0)

    def z_planes(z, b, above, below):
        link = links_at(2, z)
        ahead = colour_rows(link, above, False)
        put_kets(2, z, b, [ahead[c] - below[c] for c in range(6)])

    def own_back(z, b):
        return colour_rows(links_at(2, z), [own(z, c, b) for c in range(6)], True)

    def mid_body(t, carry):
        z = t // n_block + 1
        b = t % n_block
        above = [own(z + 1, c, b) for c in range(6)]
        z_planes(z, b, above, own_back(z - 1, b))
        return carry

    lax.fori_loop(0, (depth - 2) * n_block, mid_body, 0)

    load_s.wait()
    load_p.wait()
    half = s_ref.shape[1]
    for part in range(2):
        def st_body(cb, carry, part=part):
            c_at = pl.multiple_of(cb * 128, 128)
            for kb in range(half // 128):
                tile = s_vm[part, kb * 128:(kb + 1) * 128, pl.ds(c_at, 128)].T
                hi, lo = split(tile)
                cols = slice(part * half + kb * 128, part * half + (kb + 1) * 128)
                st_hi[pl.ds(c_at, 128), cols] = hi
                st_lo[pl.ds(c_at, 128), cols] = lo
            return carry

        lax.fori_loop(0, half // 128, st_body, 0)
    weight = jnp.where(ins_ref[0] < sink_ref[0], 1.0, 0.0).astype(F32)
    rows = p_ref.shape[1]
    for spin in range(NSPIN):
        scale = weight if spin < 2 else -weight
        re = p_vm[0, :, spin * nv:(spin + 1) * nv] * scale
        im = p_vm[1, :, spin * nv:(spin + 1) * nv] * scale
        for row, col, val in ((0, 0, re), (0, 1, -im), (1, 0, im), (1, 1, re)):
            hi, lo = split(val)
            p2_hi[spin, row * rows:(row + 1) * rows, col * nv:(col + 1) * nv] = hi
            p2_lo[spin, row * rows:(row + 1) * rows, col * nv:(col + 1) * nv] = lo

    def elemental(z):
        for copy in bra_copies[z]:
            copy.wait_recv()
        for c in range(3):
            re_hi, re_lo = split(bra[z, c])
            im_hi, im_lo = split(bra[z, 3 + c])
            for ref, re, im in ((rhs_hi, re_hi, im_hi), (rhs_lo, re_lo, im_lo)):
                left_cols = slice(c * plane, (c + 1) * plane)
                right_cols = slice((3 + c) * plane, (4 + c) * plane)
                ref[0:nv, left_cols] = re
                ref[0:nv, right_cols] = im
                ref[nv:2 * nv, left_cols] = -im
                ref[nv:2 * nv, right_cols] = re
        part = dot3(ket_hi[z], ket_lo[z], rhs_hi[...], rhs_lo[...], NT).reshape(acc.shape)
        if z == order[0]:
            acc[...] = part
        else:
            acc[...] += part

    for z in order[:-2]:
        elemental(z)

    halo_w.wait()

    def low_body(b, carry):
        above = [own(1, c, b) for c in range(6)]
        z_planes(0, b, above, [halo_dn[c, rows_of(b), :] for c in range(6)])
        return carry

    lax.fori_loop(0, n_block, low_body, 0)
    halo_v.wait()

    def high_body(b, carry):
        above = [halo_up[c, rows_of(b), :] for c in range(6)]
        z_planes(depth - 1, b, above, own_back(depth - 2, b))
        return carry

    lax.fori_loop(0, n_block, high_body, 0)
    for z in order[-2:]:
        elemental(z)

    for m in range(n_mom):
        for e in range(n_dir):
            for part in range(2):
                epart[2 * (m * n_dir + e) + part] = acc[
                    m * n_dir + dir_ref[e], :, part * nv:(part + 1) * nv]

    n_group = pairs2 // n_sp
    per_group = n_sp // 2

    def rs_copy(g, d):
        peer = (me_z + d) % n_sp
        return remote(epart.at[g * n_sp + peer], rs_buf.at[g, d - 1], rs_s.at[g, d - 1],
                      rs_r.at[g, d - 1], "space", peer)

    def ag_copy(g, d):
        return remote(e_own.at[g], e_full.at[g * n_sp + me_z, my_rows, :], ag_s.at[g, d - 1],
                      ag_r.at[g, d - 1], "space", (me_z + d) % n_sp)

    def fx_copy(g, slot, d):
        owner = (me_z + n_sp - slot) % n_sp
        target = e_full.at[g * n_sp + owner, my_rows, :]
        return remote(target if slot else e_own.at[g], target, fx_s.at[g, slot, d - 1],
                      fx_r.at[g, slot, d - 1], "tsink", (me_x + d) % n_ts)

    def reduce(g):
        total = epart[g * n_sp + me_z]
        for d in range(1, n_sp):
            rs_copy(g, d).wait_recv()
            total = total + rs_buf[g, d - 1]
        e_own[g] = total
        e_full[g * n_sp + me_z, my_rows, :] = total
        for d in range(1, n_sp):
            ag_copy(g, d).start()
        for d in range(1, n_ts):
            fx_copy(g, 0, d).start()

    def forward(g):
        for slot in range(1, n_sp):
            ag_copy(g, slot).wait_recv()
            for d in range(1, n_ts):
                fx_copy(g, slot, d).start()

    def left(g):
        for slot in range(n_sp):
            for d in range(1, n_ts):
                fx_copy(g, slot, d).wait_recv()
        for i in range(per_group):
            for part in range(2):
                hi, lo = split(e_full[g * n_sp + 2 * i + part])
                e_hi[i * nv:(i + 1) * nv, part * nv:(part + 1) * nv] = hi
                e_lo[i * nv:(i + 1) * nv, part * nv:(part + 1) * nv] = lo

        def left_body(spin, carry):
            prod = dot3(e_hi[...], e_lo[...], p2_hi[spin], p2_lo[spin], NT)
            at = pl.ds(pl.multiple_of(spin * nv, nv), nv)
            at_low = pl.ds(pl.multiple_of(half + spin * nv, nv), nv)
            for i in range(per_group):
                hi, lo = split(prod[i * nv:(i + 1) * nv])
                for ref, val in ((l2_hi, hi), (l2_lo, lo)):
                    ref[g * per_group + i, at, :] = val
                    ref[g * per_group + i, at_low, 0:rows] = -val[:, rows:]
                    ref[g * per_group + i, at_low, rows:] = val[:, :rows]
            return carry

        lax.fori_loop(0, NSPIN, left_body, 0)

    def spread(g):
        for d in range(1, n_sp):
            rs_copy(g, d).start()

    for g in range(n_group):
        spread(g)
    n_col = recv_a.shape[1]

    def right(q, pair):
        at = pl.ds(pl.multiple_of(pair * (2 * n_col), 2 * n_col), 2 * n_col)
        return dot3(st_hi[at, :], st_lo[at, :], l2_hi[q], l2_lo[q], NN)

    def copy_a(q):
        return remote(tmp_a.at[q, 1 - core], recv_a.at[q], a_s.at[q], a_r.at[q], "tins", mate)

    def copy_y(q):
        return remote(sum_a.at[q], recv_y.at[q], y_s.at[q], y_r.at[q], "tins", far)

    def copy_b(q):
        return remote(tmp_b.at[q, 1 - core], recv_b.at[q], b_s.at[q], b_r.at[q], "tins", mate)

    def relay(q):
        copy_a(q).wait_recv()
        sum_a[q] = tmp_a[q, core] + recv_a[q]
        copy_y(q).start()

    my_pair = me_t // 2

    def near(q):
        res = right(q, 1 - my_pair)
        tmp_a[q, 0] = res[:n_col]
        tmp_a[q, 1] = res[n_col:]
        copy_a(q).start()

    for g in range(n_group + 2):
        if g < n_group:
            reduce(g)
        if 1 <= g <= n_group:
            forward(g - 1)
        if g >= 2:
            left(g - 2)
            for q in range((g - 2) * per_group, (g - 1) * per_group):
                near(q)
                if q:
                    relay(q - 1)
    relay(pairs - 1)
    for q in range(pairs):
        res = right(q, my_pair)
        tmp_b[q, 0] = res[:n_col]
        tmp_b[q, 1] = res[n_col:]
        copy_b(q).start()
    for q in range(pairs):
        copy_b(q).wait_recv()
        copy_y(q).wait_recv()
        val = tmp_b[q, core] + recv_b[q] + recv_y[q]
        for part in range(2):
            out_ref[pl.ds(2 * q + part, n_col, stride=pairs2), :] = (
                val[:, part * rows:(part + 1) * rows])

    for z in order:
        for copy in bra_copies[z]:
            copy.wait_send()
    for g in range(n_group):
        for d in range(1, n_sp):
            rs_copy(g, d).wait_send()
            ag_copy(g, d).wait_send()
        for slot in range(n_sp):
            for d in range(1, n_ts):
                fx_copy(g, slot, d).wait_send()
    for q in range(pairs):
        copy_a(q).wait_send()
        copy_y(q).wait_send()
        copy_b(q).wait_send()


def pair_kernel(
    n_sp, dir_ref, mom_ref, ins_ref, sink_ref, ev_ref, link_hbm, p_ref, s_ref, out_ref,
    link_ref, cos_ref, sin_ref, p_vm, s_vm, in_sem,
    vec_own, vec_far, w_top, halo_up, halo_dn, ket_hi, ket_lo, rhs_own, rhs_far, acc_own, acc_far,
    part_own, part_far, buf_own, buf_far, sum_own, sum_far, e_full, e_two, st_two,
    p2_hi, p2_lo, l2_hi, l2_lo, tmp_a, recv_a, sum_a, tmp_b, recv_b, recv_y,
    loc_sem, v_s, v_r, halo_s, halo_r, rd_s, rd_r, gd_s, gd_r, xd_s, xd_r,
    rf_s, rf_r, gf_s, gf_r, xf_s, xf_r, a_s, a_r, y_s, y_r, b_s, b_r,
):
    _, vecs, depth, plane = ev_ref.shape
    pairs = part_own.shape[1]
    n_dir = 3
    n_mom = pairs // n_dir
    nv = 2 * vecs
    me_x = lax.axis_index("tsink")
    me_z = lax.axis_index("space")
    me_t = lax.axis_index("tins")
    core = me_t % 2
    mate = me_t + 1 - 2 * core
    far = (me_t + 2) % 4
    up = (me_z + 1) % n_sp
    down = (me_z + n_sp - 1) % n_sp
    other = 1 - me_x
    is_head = me_x == core
    not_head = me_x != core

    barrier = pltpu.get_barrier_semaphore()
    mesh_type = pl.DeviceIdType.MESH
    pl.semaphore_signal(barrier, inc=1, device_id={"tsink": other}, device_id_type=mesh_type)
    for d in range(1, n_sp):
        pl.semaphore_signal(barrier, inc=1, device_id={"space": (me_z + d) % n_sp},
                            device_id_type=mesh_type)
    for target in (mate, far):
        pl.semaphore_signal(barrier, inc=1, device_id={"tins": target}, device_id_type=mesh_type)
    local = [
        pltpu.make_async_copy(ev_ref.at[:, :, z, :], vec_own.at[z], loc_sem.at[z])
        for z in range(depth)
    ]
    local[depth - 1].start()
    load_links = pltpu.make_async_copy(link_hbm, link_ref, in_sem.at[2])
    load_links.start()
    for copy in local[:-1]:
        copy.start()
    load_p = pltpu.make_async_copy(p_ref, p_vm, in_sem.at[0])
    load_s = pltpu.make_async_copy(s_ref, s_vm, in_sem.at[1])
    load_p.start()
    load_s.start()
    pl.semaphore_wait(barrier, 1 + n_sp - 1 + 2)

    order = list(range(1, depth - 1)) + [0, depth - 1]
    vec_copies = {
        z: remote(ev_ref.at[:, :, z, :], vec_far.at[z], v_s.at[z], v_r.at[z], "tsink", other)
        for z in order
    }
    halo_v = remote(ev_ref.at[:, :, 0, :], halo_up, halo_s.at[0], halo_r.at[0], "space", down)
    halo_w = remote(w_top, halo_dn, halo_s.at[1], halo_r.at[1], "space", up)

    @pl.when(is_head)
    def _():
        halo_v.start()

    @pl.when(not_head)
    def _():
        for z in order:
            vec_copies[z].start()
        halo_dn[...] = jnp.zeros_like(halo_dn)

    block = min(16, vecs)
    n_block = vecs // block

    def rows_of(b):
        return pl.ds(pl.multiple_of(b * block, block), block)

    def own(z, c, b):
        return vec_own[z, c, rows_of(b), :]

    def links_at(k, z):
        return [
            [[link_ref[k, part, i, j, pl.ds(z, 1), :] for j in range(3)] for i in range(3)]
            for part in range(2)
        ]

    column = lax.broadcasted_iota(jnp.int32, (block, plane), 1) % L

    def shifted(x, k, sign):
        if k == 1:
            return pltpu.roll(x, plane - L if sign > 0 else L, axis=1)
        if sign > 0:
            return jnp.where(column == L - 1, pltpu.roll(x, L - 1, axis=1),
                             pltpu.roll(x, plane - 1, axis=1))
        return jnp.where(column == 0, pltpu.roll(x, plane + 1 - L, axis=1),
                         pltpu.roll(x, 1, axis=1))

    site = lax.broadcasted_iota(jnp.int32, (depth, plane), 1)
    z_coord = me_z * depth + lax.broadcasted_iota(jnp.int32, (depth, plane), 0)
    for m in range(n_mom):
        product = mom_ref[m, 0] * (site % L) + mom_ref[m, 1] * (site // L) + mom_ref[m, 2] * z_coord
        steps = [0] + [mom_ref[m, k] for k in range(n_dir)] + [-mom_ref[m, k] for k in range(n_dir)]
        for j, step in enumerate(steps):
            angles = (2.0 * math.pi / L) * jnp.bitwise_and(product + step, L - 1).astype(F32)
            cos_ref[m, j] = jnp.cos(angles)
            sin_ref[m, j] = jnp.sin(angles)

    def put_kets(k, z, b, ahead, back, turned):
        deriv = [ahead[c] - back[c] for c in range(6)]

        def put(start, i, re, im):
            at = pl.multiple_of(start * vecs + b * block, block)
            for comp, val in ((i, re), (3 + i, im)):
                hi, lo = split(val)
                cols = slice(comp * plane, (comp + 1) * plane)
                ket_hi[z, pl.ds(at, block), cols] = hi
                ket_lo[z, pl.ds(at, block), cols] = lo

        for m in range(n_mom):
            c, c_up, c_dn = [cos_ref[m, j, pl.ds(z, 1), :] for j in (0, 1 + k, 1 + n_dir + k)]
            s, s_up, s_dn = [sin_ref[m, j, pl.ds(z, 1), :] for j in (0, 1 + k, 1 + n_dir + k)]
            for i in range(3):
                put(m * n_dir + k, i, c * deriv[i] + s * deriv[3 + i],
                    c * deriv[3 + i] - s * deriv[i])
                if not turned:
                    continue
                re = c_up * ahead[i] - s_up * ahead[3 + i]
                im = c_up * ahead[3 + i] + s_up * ahead[i]
                if turned == 2:
                    re = re - c_dn * back[i] + s_dn * back[3 + i]
                    im = im - c_dn * back[3 + i] - s_dn * back[i]
                put(pairs + m * n_dir + k, i, re, im)

    def by_role(count, body, head_turned, turned):
        @pl.when(is_head)
        def _():
            lax.fori_loop(0, count, functools.partial(body, head_turned), 0)

        @pl.when(not_head)
        def _():
            lax.fori_loop(0, count, functools.partial(body, turned), 0)

    load_links.wait()
    local[depth - 1].wait()

    def top_body(b, carry):
        vec = [own(depth - 1, c, b) for c in range(6)]
        w = colour_rows(links_at(2, depth - 1), vec, True)
        for c in range(6):
            w_top[c, rows_of(b), :] = w[c]
        return carry

    @pl.when(is_head)
    def _():
        lax.fori_loop(0, n_block, top_body, 0)
        halo_w.start()

    @pl.when(not_head)
    def _():
        halo_v.start()

    for copy in local[:-1]:
        copy.wait()

    for k in range(2):
        def xy_body(turned, t, carry, k=k):
            z = t // n_block
            b = t % n_block
            vec = [own(z, c, b) for c in range(6)]
            link = links_at(k, z)
            ahead = colour_rows(link, [shifted(x, k, 1) for x in vec], False)
            back = colour_rows(link, vec, True)
            put_kets(k, z, b, ahead, [shifted(x, k, -1) for x in back], turned)
            return carry

        by_role(depth * n_block, xy_body, 2, 0)

    def z_planes(z, b, above, below, turned):
        put_kets(2, z, b, colour_rows(links_at(2, z), above, False), below, turned)

    def own_back(z, b):
        return colour_rows(links_at(2, z), [own(z, c, b) for c in range(6)], True)

    def mid_body(turned, t, carry):
        z = t // n_block + 1
        b = t % n_block
        z_planes(z, b, [own(z + 1, c, b) for c in range(6)], own_back(z - 1, b),
                 turned)
        return carry

    by_role((depth - 2) * n_block, mid_body, 2, 0)

    def fill(rhs, vec, z):
        for c in range(3):
            left_cols = slice(c * plane, (c + 1) * plane)
            right_cols = slice((3 + c) * plane, (4 + c) * plane)
            for at, re, im in zip((0, nv), split(vec[z, c]), split(vec[z, 3 + c])):
                rhs[at:at + vecs, left_cols] = re
                rhs[at:at + vecs, right_cols] = im
                rhs[at + vecs:at + nv, left_cols] = -im
                rhs[at + vecs:at + nv, right_cols] = re

    def elemental(z, rhs, acc, start):
        rows = pairs * vecs
        both = lax.dot_general(ket_hi[z, start:start + rows, :], rhs[...], NT,
                               preferred_element_type=F32)
        low = lax.dot_general(ket_lo[z, start:start + rows, :], rhs[0:nv, :], NT,
                              preferred_element_type=F32)
        part = (both[:, :nv] + both[:, nv:] + low).reshape(pairs, vecs, nv)
        at = slice(start // vecs, start // vecs + pairs)
        if z == order[0]:
            acc[at] = part
        else:
            acc[at] += part

    def own_elemental(z):
        fill(rhs_own, vec_own, z)
        elemental(z, rhs_own, acc_own, 0)

    def far_elemental(z):
        @pl.when(is_head)
        def _():
            vec_copies[z].wait_recv()
            fill(rhs_far, vec_far, z)
            for start in (0, pairs * vecs):
                elemental(z, rhs_far, acc_far, start)

    for z in order[:-2]:
        own_elemental(z)

    load_s.wait()
    load_p.wait()
    half = s_ref.shape[1]
    wide = half // 2
    for part in range(2):
        def st_body(cb, carry, part=part):
            c_at = pl.multiple_of(cb * 128, 128)
            for kb in range(half // nv):
                near_at = pl.multiple_of(kb * nv + core * vecs, vecs)
                far_at = pl.multiple_of(kb * nv + (1 - core) * vecs, vecs)
                tile = jnp.concatenate([s_vm[part, pl.ds(near_at, vecs), pl.ds(c_at, 128)],
                                        s_vm[part, pl.ds(far_at, vecs), pl.ds(c_at, 128)]], axis=0).T
                hi, lo = split(tile)
                cols = slice(part * half + kb * nv, part * half + (kb + 1) * nv)
                at = pl.multiple_of(cb // 2 * (2 * wide) + cb % 2 * 128, 128)
                st_two[pl.ds(at, 128), cols] = hi
                st_two[pl.ds(at + wide, 128), cols] = lo
            return carry

        lax.fori_loop(0, half // 128, st_body, 0)
    weight = jnp.where(ins_ref[0] < sink_ref[0], 1.0, 0.0).astype(F32)
    rows = p_ref.shape[1]
    low_lane = lax.broadcasted_iota(jnp.int32, (rows, nv), 1) < vecs
    for spin in range(NSPIN):
        scale = weight if spin < 2 else -weight
        re = p_vm[0, :, spin * nv:(spin + 1) * nv] * scale
        im = p_vm[1, :, spin * nv:(spin + 1) * nv] * scale
        re_roll = pltpu.roll(re, vecs, axis=1)
        im_roll = pltpu.roll(im, vecs, axis=1)
        re, re_roll = jnp.where(core == 0, re, re_roll), jnp.where(core == 0, re_roll, re)
        im, im_roll = jnp.where(core == 0, im, im_roll), jnp.where(core == 0, im_roll, im)
        for row, (x, x_roll, y, y_roll) in enumerate(((re, re_roll, -im, -im_roll),
                                                      (im, im_roll, re, re_roll))):
            for col, val in enumerate((jnp.where(low_lane, x, y_roll), jnp.where(low_lane, x_roll, y))):
                hi, lo = split(val)
                p2_hi[spin, row * rows:(row + 1) * rows, col * nv:(col + 1) * nv] = hi
                p2_lo[spin, row * rows:(row + 1) * rows, col * nv:(col + 1) * nv] = lo

    @pl.when(is_head)
    def _():
        halo_w.wait()

    def low_body(turned, b, carry):
        above = [own(1, c, b) for c in range(6)]
        z_planes(0, b, above, [halo_dn[c, rows_of(b), :] for c in range(6)], turned)
        return carry

    by_role(n_block, low_body, 2, 0)
    halo_v.wait()

    def high_body(turned, b, carry):
        above = [halo_up[c, rows_of(b), :] for c in range(6)]
        z_planes(depth - 1, b, above, own_back(depth - 2, b), turned)
        return carry

    by_role(n_block, high_body, 2, 1)
    for z in order[-2:]:
        own_elemental(z)

    def turn(val):
        flat = val.T
        return jnp.concatenate([-flat[:vecs], flat[vecs:]], axis=1)

    @pl.when(not_head)
    def _():
        for m in range(n_mom):
            q = m * n_dir + n_dir - 1
            at = slice((pairs + q) * vecs, (pairs + q + 1) * vecs)
            both = lax.dot_general(ket_hi[depth - 1, at, :], rhs_own[...], NT,
                                   preferred_element_type=F32)
            low = lax.dot_general(ket_lo[depth - 1, at, :], rhs_own[0:nv, :], NT,
                                  preferred_element_type=F32)
            acc_own[q] += turn(both[:, :nv] + both[:, nv:] + low)

    strip = vecs // n_sp
    per_group = part_far.shape[2]
    n_group = pairs // per_group
    my_strip = pl.ds(pl.multiple_of(me_z * strip, strip), strip)
    corner = jnp.where(is_head, 0, 3)

    def chosen(acc, q, base):
        return acc[base + (q // n_dir) * n_dir + dir_ref[q % n_dir]]

    def strips(val):
        return [val[z * strip:(z + 1) * strip, :] for z in range(n_sp)]

    for q in range(pairs):
        for z, val in enumerate(strips(chosen(acc_own, q, 0))):
            part_own[z, q] = val

    def rd_copy(d):
        peer = (me_z + d) % n_sp
        return remote(part_own.at[peer], buf_own.at[d - 1], rd_s.at[d - 1], rd_r.at[d - 1],
                      "space", peer)

    def gd_copy(d):
        return remote(sum_own, e_full.at[:, corner, my_strip, :], gd_s.at[d - 1], gd_r.at[d - 1],
                      "space", (me_z + d) % n_sp)

    def xd_copy(g):
        block_at = e_full.at[pl.ds(g * per_group, per_group), corner]
        return remote(block_at, block_at, xd_s.at[g], xd_r.at[g], "tsink", other)

    def rf_copy(g, d):
        peer = (me_z + d) % n_sp
        return remote(part_far.at[g, peer], buf_far.at[g, d - 1], rf_s.at[g, d - 1],
                      rf_r.at[g, d - 1], "space", peer)

    def mixed(g, strip_at):
        return e_full.at[pl.ds(g * per_group, per_group), pl.ds(1, 2), strip_at, :]

    def gf_copy(g, d):
        return remote(sum_far.at[g], mixed(g, my_strip), gf_s.at[g, d - 1], gf_r.at[g, d - 1],
                      "space", (me_z + d) % n_sp)

    def xf_copy(g, slot):
        return pltpu.make_async_remote_copy(
            src_ref=sum_far.at[g], dst_ref=mixed(g, my_strip), send_sem=xf_s.at[g, slot],
            recv_sem=xf_r.at[g, slot], device_id={"tsink": other, "space": (me_z + slot) % n_sp},
            device_id_type=pl.DeviceIdType.MESH)

    for d in range(1, n_sp):
        rd_copy(d).start()
    for z in order[:-1]:
        far_elemental(z)
    total = part_own[me_z]
    for d in range(1, n_sp):
        rd_copy(d).wait_recv()
        total = total + buf_own[d - 1]
    sum_own[...] = total
    e_full[:, corner, my_strip, :] = total
    for d in range(1, n_sp):
        gd_copy(d).start()
    far_elemental(order[-1])

    @pl.when(is_head)
    def _():
        for q in range(pairs):
            g, i = q // per_group, q % per_group
            for z, val in enumerate(strips(chosen(acc_far, q, 0))):
                part_far[g, z, i, 0] = val
            for z, val in enumerate(strips(turn(chosen(acc_far, q, pairs)))):
                part_far[g, z, i, 1] = val
            if i == per_group - 1:
                for d in range(1, n_sp):
                    rf_copy(g, d).start()

    @pl.when(not_head)
    def _():
        for z in order:
            vec_copies[z].wait_send()

    def reduce(g):
        @pl.when(is_head)
        def _():
            total = part_far[g, me_z]
            for d in range(1, n_sp):
                rf_copy(g, d).wait_recv()
                total = total + buf_far[g, d - 1]
            sum_far[g] = total
            e_full[pl.ds(g * per_group, per_group), pl.ds(1, 2), my_strip, :] = total
            for d in range(1, n_sp):
                gf_copy(g, d).start()
            for slot in range(n_sp):
                xf_copy(g, slot).start()

    def forward(g):
        @pl.when(is_head)
        def _():
            for d in range(1, n_sp):
                gf_copy(g, d).wait_recv()

    def left(g):
        xd_copy(g).wait_recv()

        @pl.when(not_head)
        def _():
            for slot in range(n_sp):
                xf_copy(g, slot).wait_recv()

        for i in range(per_group):
            for quad in range(4):
                hi, lo = split(e_full[g * per_group + i, quad])
                at = i * nv + quad // 2 * vecs
                low_at = at + per_group * nv
                cols = slice(quad % 2 * nv, (quad % 2 + 1) * nv)
                e_two[at:at + vecs, cols] = hi
                e_two[low_at:low_at + vecs, cols] = lo

        def left_body(spin, carry):
            prod = dot_two(e_two[...], p2_hi[spin], p2_lo[spin], NT)
            at = pl.ds(pl.multiple_of(spin * nv, nv), nv)
            at_low = pl.ds(pl.multiple_of(half + spin * nv, nv), nv)
            for i in range(per_group):
                hi, lo = split(prod[i * nv:(i + 1) * nv])
                for ref, val in ((l2_hi, hi), (l2_lo, lo)):
                    ref[g * per_group + i, at, :] = val
                    ref[g * per_group + i, at_low, 0:rows] = -val[:, rows:]
                    ref[g * per_group + i, at_low, rows:] = val[:, :rows]
            return carry

        lax.fori_loop(0, NSPIN, left_body, 0)

    n_col = recv_a.shape[1]

    def right(q, pair):
        at = pl.ds(pl.multiple_of(pair * (2 * wide), 2 * wide), 2 * wide)
        return dot_two(st_two[at, :], l2_hi[q], l2_lo[q], NN)

    def copy_a(q):
        return remote(tmp_a.at[q, 1 - core], recv_a.at[q], a_s.at[q], a_r.at[q], "tins", mate)

    def copy_y(q):
        return remote(sum_a.at[q], recv_y.at[q], y_s.at[q], y_r.at[q], "tins", far)

    def copy_b(q):
        return remote(tmp_b.at[q, 1 - core], recv_b.at[q], b_s.at[q], b_r.at[q], "tins", mate)

    def relay(q):
        copy_a(q).wait_recv()
        sum_a[q] = tmp_a[q, core] + recv_a[q]
        copy_y(q).start()

    my_pair = me_t // 2

    def near(q):
        res = right(q, 1 - my_pair)
        tmp_a[q, 0] = res[:n_col]
        tmp_a[q, 1] = res[n_col:]
        copy_a(q).start()

    for g in range(n_group):
        reduce(g)
        if g == min(1, n_group - 1):
            for d in range(1, n_sp):
                gd_copy(d).wait_recv()
            for h in range(n_group):
                xd_copy(h).start()
    for g in range(n_group):
        forward(g)
        left(g)
        for q in range(g * per_group, (g + 1) * per_group):
            near(q)
            if q:
                relay(q - 1)
    relay(pairs - 1)
    for q in range(pairs):
        res = right(q, my_pair)
        tmp_b[q, 0] = res[:n_col]
        tmp_b[q, 1] = res[n_col:]
        copy_b(q).start()
    for q in range(pairs):
        copy_b(q).wait_recv()
        copy_y(q).wait_recv()
        val = tmp_b[q, core] + recv_b[q] + recv_y[q]
        for part in range(2):
            out_ref[pl.ds(2 * q + part, n_col, stride=2 * pairs), :] = (
                val[:, part * rows:(part + 1) * rows])

    for d in range(1, n_sp):
        rd_copy(d).wait_send()
        gd_copy(d).wait_send()

    @pl.when(is_head)
    def _():
        for g in range(n_group):
            for d in range(1, n_sp):
                rf_copy(g, d).wait_send()
                gf_copy(g, d).wait_send()
            for slot in range(n_sp):
                xf_copy(g, slot).wait_send()

    for g in range(n_group):
        xd_copy(g).wait_send()
    for q in range(pairs):
        copy_a(q).wait_send()
        copy_y(q).wait_send()
        copy_b(q).wait_send()


def copy_kernel(in_ref, out_ref):
    out_ref[...] = in_ref[...]


def ring_call(n_ts, n_sp, n_ti, eigvecs, links, momenta, directions, ins_time, sink_time,
              sink_peramb, source_peramb):
    assert n_ti == 4
    _, _, _, vecs, depth, plane = eigvecs.shape
    nv = vecs * n_ts
    ev = eigvecs.reshape(6, vecs, depth, plane)
    pairs = momenta.shape[0] * directions.shape[0]
    order_m = source_peramb.shape[-1]
    rows = sink_peramb.shape[3]
    n_col = order_m // n_ti
    n_group = 2 * pairs // n_sp
    v = pltpu.VMEM
    dma = pltpu.SemaphoreType.DMA
    scratch = [
        v((momenta.shape[0], depth, plane), F32), v((momenta.shape[0], depth, plane), F32),
        v(sink_peramb.shape[2:], F32), v(source_peramb.shape[1:], F32), dma((2,)),
        v((depth, 6, nv, plane), F32),
        v((6, vecs, plane), F32), v((6, vecs, plane), F32), v((6, vecs, plane), F32),
        v((depth, pairs * vecs, 6 * plane), BF16), v((depth, pairs * vecs, 6 * plane), BF16),
        v((2 * nv, 6 * plane), BF16), v((2 * nv, 6 * plane), BF16),
        v((pairs, vecs, 2 * nv), F32),
        v((2 * pairs, vecs, nv), F32),
        v((n_group, n_sp - 1, vecs, nv), F32),
        v((n_group, vecs, nv), F32),
        v((2 * pairs, nv, nv), F32),
        v((n_sp // 2 * nv, 2 * nv), BF16), v((n_sp // 2 * nv, 2 * nv), BF16),
        v((order_m, 2 * order_m), BF16), v((order_m, 2 * order_m), BF16),
        v((NSPIN, 2 * rows, 2 * nv), BF16), v((NSPIN, 2 * rows, 2 * nv), BF16),
        v((pairs, 2 * order_m, 2 * rows), BF16), v((pairs, 2 * order_m, 2 * rows), BF16),
        v((pairs, 2, n_col, 2 * rows), F32),
        v((pairs, n_col, 2 * rows), F32), v((pairs, n_col, 2 * rows), F32),
        v((pairs, 2, n_col, 2 * rows), F32),
        v((pairs, n_col, 2 * rows), F32), v((pairs, n_col, 2 * rows), F32),
        dma((depth,)), dma((depth, n_ts - 1)), dma((depth, n_ts - 1)), dma((2,)), dma((2,)),
        dma((n_group, n_sp - 1)), dma((n_group, n_sp - 1)),
        dma((n_group, n_sp - 1)), dma((n_group, n_sp - 1)),
        dma((n_group, n_sp, n_ts - 1)), dma((n_group, n_sp, n_ts - 1)),
        dma((pairs,)), dma((pairs,)), dma((pairs,)), dma((pairs,)), dma((pairs,)), dma((pairs,)),
    ]
    smem = pl.BlockSpec(memory_space=pltpu.SMEM)
    vmem = pl.BlockSpec(memory_space=pltpu.VMEM)
    hbm = pl.BlockSpec(memory_space=pl.ANY)
    out = pl.pallas_call(
        functools.partial(ring_kernel, n_ts, n_sp),
        out_shape=jax.ShapeDtypeStruct((n_col * pairs * 2, rows), F32),
        in_specs=[smem] * 4 + [hbm, vmem, hbm, hbm],
        out_specs=vmem,
        scratch_shapes=scratch,
        compiler_params=pltpu.CompilerParams(
            collective_id=0, has_side_effects=True, vmem_limit_bytes=60 * 1024 * 1024
        ),
        name="peramb",
    )(directions, momenta, ins_time, sink_time, ev, links[0], sink_peramb[0, 0],
      source_peramb[0])
    tile = pl.BlockSpec((out.shape[0] // 2, rows), lambda i: (i, 0))
    out = pl.pallas_call(
        copy_kernel,
        grid=(2,),
        out_shape=jax.ShapeDtypeStruct(out.shape, F32),
        in_specs=[tile],
        out_specs=tile,
        name="result",
    )(out)
    return out.reshape(n_col, 1, pairs, 2, rows)


def pair_call(n_ts, n_sp, n_ti, eigvecs, links, momenta, directions, ins_time, sink_time,
              sink_peramb, source_peramb):
    assert n_ts == 2 and n_ti == 4
    _, _, _, vecs, depth, plane = eigvecs.shape
    nv = vecs * n_ts
    ev = eigvecs.reshape(6, vecs, depth, plane)
    n_mom = momenta.shape[0]
    pairs = n_mom * directions.shape[0]
    order_m = source_peramb.shape[-1]
    rows = sink_peramb.shape[3]
    n_col = order_m // n_ti
    per_group = 1
    n_group = pairs // per_group
    strip = vecs // n_sp
    v = pltpu.VMEM
    dma = pltpu.SemaphoreType.DMA
    scratch = [
        v(links.shape[1:], F32), v((n_mom, 7, depth, plane), F32), v((n_mom, 7, depth, plane), F32),
        v(sink_peramb.shape[2:], F32), v(source_peramb.shape[1:], F32), dma((3,)),
        v((depth, 6, vecs, plane), F32), v((depth, 6, vecs, plane), F32),
        v((6, vecs, plane), F32), v((6, vecs, plane), F32), v((6, vecs, plane), F32),
        v((depth, 2 * pairs * vecs, 6 * plane), BF16), v((depth, 2 * pairs * vecs, 6 * plane), BF16),
        v((2 * nv, 6 * plane), BF16), v((2 * nv, 6 * plane), BF16),
        v((pairs, vecs, nv), F32), v((2 * pairs, vecs, nv), F32),
        v((n_sp, pairs, strip, nv), F32), v((n_group, n_sp, per_group, 2, strip, nv), F32),
        v((n_sp - 1, pairs, strip, nv), F32), v((n_group, n_sp - 1, per_group, 2, strip, nv), F32),
        v((pairs, strip, nv), F32), v((n_group, per_group, 2, strip, nv), F32),
        v((pairs, 4, vecs, nv), F32),
        v((2 * per_group * nv, 2 * nv), BF16), v((2 * order_m, 2 * order_m), BF16),
        v((NSPIN, 2 * rows, 2 * nv), BF16), v((NSPIN, 2 * rows, 2 * nv), BF16),
        v((pairs, 2 * order_m, 2 * rows), BF16), v((pairs, 2 * order_m, 2 * rows), BF16),
        v((pairs, 2, n_col, 2 * rows), F32),
        v((pairs, n_col, 2 * rows), F32), v((pairs, n_col, 2 * rows), F32),
        v((pairs, 2, n_col, 2 * rows), F32),
        v((pairs, n_col, 2 * rows), F32), v((pairs, n_col, 2 * rows), F32),
        dma((depth,)), dma((depth,)), dma((depth,)), dma((2,)), dma((2,)),
        dma((n_sp - 1,)), dma((n_sp - 1,)), dma((n_sp - 1,)), dma((n_sp - 1,)),
        dma((n_group,)), dma((n_group,)),
        dma((n_group, n_sp - 1)), dma((n_group, n_sp - 1)),
        dma((n_group, n_sp - 1)), dma((n_group, n_sp - 1)),
        dma((n_group, n_sp)), dma((n_group, n_sp)),
        dma((pairs,)), dma((pairs,)), dma((pairs,)), dma((pairs,)), dma((pairs,)), dma((pairs,)),
    ]
    smem = pl.BlockSpec(memory_space=pltpu.SMEM)
    vmem = pl.BlockSpec(memory_space=pltpu.VMEM)
    hbm = pl.BlockSpec(memory_space=pl.ANY)
    out = pl.pallas_call(
        functools.partial(pair_kernel, n_sp),
        out_shape=jax.ShapeDtypeStruct((n_col * pairs * 2, rows), F32),
        in_specs=[smem] * 4 + [hbm] * 4,
        out_specs=vmem,
        scratch_shapes=scratch,
        compiler_params=pltpu.CompilerParams(
            collective_id=0, has_side_effects=True, vmem_limit_bytes=60 * 1024 * 1024
        ),
        name="peramb",
    )(directions, momenta, ins_time, sink_time, ev, links[0], sink_peramb[0, 0],
      source_peramb[0])
    tile = pl.BlockSpec((out.shape[0] // 2, rows), lambda i: (i, 0))
    out = pl.pallas_call(
        copy_kernel,
        grid=(2,),
        out_shape=jax.ShapeDtypeStruct(out.shape, F32),
        in_specs=[tile],
        out_specs=tile,
        name="result",
    )(out)
    return out.reshape(n_col, 1, pairs, 2, rows)


def solution(mesh):
    in_specs = (
        P("tins", None, None, "tsink", "space", None),
        P("tins", None, None, None, None, "space", None),
        P(),
        P(),
        P("tins"),
        P("tsink"),
        P("tsink", "tins", None, "space", None),
        P("tins", None, None, None),
    )
    out_specs = P("tins", "tsink", None, None, "space")
    sizes = mesh.shape["tsink"], mesh.shape["space"], mesh.shape["tins"]
    body = functools.partial(pair_call if sizes[0] == 2 else ring_call, *sizes)
    return jax.shard_map(body, mesh=mesh, in_specs=in_specs, out_specs=out_specs, check_vma=False)
```

```python
import functools
import math

import jax
import jax.numpy as jnp
from jax import lax
from jax.experimental import pallas as pl
from jax.experimental.pallas import tpu as pltpu
from jax.sharding import PartitionSpec as P

L = 16
NSPIN = 4
BF16 = jnp.bfloat16
F32 = jnp.float32
NT = (((1,), (1,)), ((), ()))
NN = (((1,), (0,)), ((), ()))


def split(x):
    hi = x.astype(BF16)
    return hi, (x - hi.astype(F32)).astype(BF16)


def dot3(a_hi, a_lo, b_hi, b_lo, dims):
    def one(a, b):
        return lax.dot_general(a, b, dims, preferred_element_type=F32)

    return one(a_hi, b_hi) + one(a_hi, b_lo) + one(a_lo, b_hi)


def dot_two(a, b_hi, b_lo, dims):
    rows = a.shape[0] // 2
    both = lax.dot_general(a, b_hi, dims, preferred_element_type=F32)
    low = lax.dot_general(a[:rows], b_lo, dims, preferred_element_type=F32)
    return both[:rows] + both[rows:] + low


def remote(src, dst, send, recv, axis, index):
    return pltpu.make_async_remote_copy(
        src_ref=src,
        dst_ref=dst,
        send_sem=send,
        recv_sem=recv,
        device_id={axis: index},
        device_id_type=pl.DeviceIdType.MESH,
    )


def colour_rows(link, vec, adjoint):
    rows = []
    for i in range(3):
        re = im = None
        for j in range(3):
            if adjoint:
                a, b = link[0][j][i], link[1][j][i]
                tr = a * vec[j] + b * vec[3 + j]
                ti = a * vec[3 + j] - b * vec[j]
            else:
                a, b = link[0][i][j], link[1][i][j]
                tr = a * vec[j] - b * vec[3 + j]
                ti = a * vec[3 + j] + b * vec[j]
            re = tr if re is None else re + tr
            im = ti if im is None else im + ti
        rows.append((re, im))
    return [r[0] for r in rows] + [r[1] for r in rows]


def ring_kernel(
    n_ts, n_sp, dir_ref, mom_ref, ins_ref, sink_ref, ev_ref, link_ref, p_ref, s_ref, out_ref,
    cos_ref, sin_ref, p_vm, s_vm, in_sem,
    bra, w_top, halo_up, halo_dn, ket_hi, ket_lo, rhs_hi, rhs_lo, acc, epart, rs_buf, e_own,
    e_full, e_hi, e_lo, st_hi, st_lo, p2_hi, p2_lo, l2_hi, l2_lo, tmp_a, recv_a, sum_a, tmp_b,
    recv_b, recv_y, loc_sem, bra_s, bra_r, halo_s, halo_r, rs_s, rs_r, ag_s, ag_r, fx_s, fx_r,
    a_s, a_r, y_s, y_r, b_s, b_r,
):
    _, vecs, depth, plane = ev_ref.shape
    pairs2 = epart.shape[0]
    pairs = pairs2 // 2
    n_dir = 3
    n_mom = pairs // n_dir
    nv = bra.shape[2]
    me_x = lax.axis_index("tsink")
    me_z = lax.axis_index("space")
    me_t = lax.axis_index("tins")
    core = me_t % 2
    mate = me_t + 1 - 2 * core
    far = (me_t + 2) % 4
    up = (me_z + 1) % n_sp
    down = (me_z + n_sp - 1) % n_sp
    my_rows = pl.ds(pl.multiple_of(me_x * vecs, vecs), vecs)
    local = [
        pltpu.make_async_copy(ev_ref.at[:, :, z, :], bra.at[z, :, my_rows, :], loc_sem.at[z])
        for z in range(depth)
    ]
    for copy in reversed(local):
        copy.start()
    load_p = pltpu.make_async_copy(p_ref, p_vm, in_sem.at[0])
    load_s = pltpu.make_async_copy(s_ref, s_vm, in_sem.at[1])
    load_p.start()
    load_s.start()
    barrier = pltpu.get_barrier_semaphore()
    mesh_type = pl.DeviceIdType.MESH
    for d in range(1, n_ts):
        pl.semaphore_signal(barrier, inc=1, device_id={"tsink": (me_x + d) % n_ts},
                            device_id_type=mesh_type)
    for d in range(1, n_sp):
        pl.semaphore_signal(barrier, inc=1, device_id={"space": (me_z + d) % n_sp},
                            device_id_type=mesh_type)
    for target in (mate, far):
        pl.semaphore_signal(barrier, inc=1, device_id={"tins": target}, device_id_type=mesh_type)
    pl.semaphore_wait(barrier, n_ts - 1 + n_sp - 1 + 2)

    order = list(range(1, depth - 1)) + [0, depth - 1]
    bra_copies = {}
    for z in order:
        bra_copies[z] = [
            remote(ev_ref.at[:, :, z, :], bra.at[z, :, my_rows, :], bra_s.at[z, d - 1], bra_r.at[z, d - 1],
                   "tsink", (me_x + d) % n_ts)
            for d in range(1, n_ts)
        ]
    halo_v = remote(ev_ref.at[:, :, 0, :], halo_up, halo_s.at[0], halo_r.at[0], "space", down)
    halo_w = remote(w_top, halo_dn, halo_s.at[1], halo_r.at[1], "space", up)
    halo_v.start()
    for z in order:
        for copy in bra_copies[z]:
            copy.start()

    block = min(16, vecs)
    n_block = vecs // block

    def rows_of(b):
        return pl.ds(pl.multiple_of(b * block, block), block)

    def own(z, c, b):
        return bra[z, c, pl.ds(pl.multiple_of(me_x * vecs + b * block, block), block), :]

    def links_at(k, z):
        return [
            [[link_ref[k, part, i, j, pl.ds(z, 1), :] for j in range(3)] for i in range(3)]
            for part in range(2)
        ]

    column = lax.broadcasted_iota(jnp.int32, (block, plane), 1) % L

    def shifted(x, k, sign):
        if k == 1:
            return pltpu.roll(x, plane - L if sign > 0 else L, axis=1)
        if sign > 0:
            return jnp.where(column == L - 1, pltpu.roll(x, L - 1, axis=1),
                             pltpu.roll(x, plane - 1, axis=1))
        return jnp.where(column == 0, pltpu.roll(x, plane + 1 - L, axis=1),
                         pltpu.roll(x, 1, axis=1))

    site = lax.broadcasted_iota(jnp.int32, (depth, plane), 1)
    z_coord = me_z * depth + lax.broadcasted_iota(jnp.int32, (depth, plane), 0)
    for m in range(n_mom):
        product = mom_ref[m, 0] * (site % L) + mom_ref[m, 1] * (site // L) + mom_ref[m, 2] * z_coord
        angles = (2.0 * math.pi / L) * jnp.bitwise_and(product, L - 1).astype(F32)
        cos_ref[m] = jnp.cos(angles)
        sin_ref[m] = jnp.sin(angles)

    def put_kets(k, z, b, deriv):
        for m in range(n_mom):
            c = cos_ref[m, pl.ds(z, 1), :]
            s = sin_ref[m, pl.ds(z, 1), :]
            start = pl.multiple_of((m * n_dir + k) * vecs + b * block, block)
            for i in range(3):
                for comp, val in (
                    (i, c * deriv[i] + s * deriv[3 + i]),
                    (3 + i, c * deriv[3 + i] - s * deriv[i]),
                ):
                    hi, lo = split(val)
                    cols = slice(comp * plane, (comp + 1) * plane)
                    ket_hi[z, pl.ds(start, block), cols] = hi
                    ket_lo[z, pl.ds(start, block), cols] = lo

    local[depth - 1].wait()

    def top_body(b, carry):
        vec = [own(depth - 1, c, b) for c in range(6)]
        w = colour_rows(links_at(2, depth - 1), vec, True)
        for c in range(6):
            w_top[c, rows_of(b), :] = w[c]
        return carry

    lax.fori_loop(0, n_block, top_body, 0)
    halo_w.start()
    for copy in local[:-1]:
        copy.wait()

    for k in range(2):
        def xy_body(t, carry, k=k):
            z = t // n_block
            b = t % n_block
            vec = [own(z, c, b) for c in range(6)]
            link = links_at(k, z)
            ahead = colour_rows(link, [shifted(x, k, 1) for x in vec], False)
            back = colour_rows(link, vec, True)
            put_kets(k, z, b, [ahead[c] - shifted(back[c], k, -1) for c in range(6)])
            return carry

        lax.fori_loop(0, depth * n_block, xy_body, 0)

    def z_planes(z, b, above, below):
        link = links_at(2, z)
        ahead = colour_rows(link, above, False)
        put_kets(2, z, b, [ahead[c] - below[c] for c in range(6)])

    def own_back(z, b):
        return colour_rows(links_at(2, z), [own(z, c, b) for c in range(6)], True)

    def mid_body(t, carry):
        z = t // n_block + 1
        b = t % n_block
        above = [own(z + 1, c, b) for c in range(6)]
        z_planes(z, b, above, own_back(z - 1, b))
        return carry

    lax.fori_loop(0, (depth - 2) * n_block, mid_body, 0)

    load_s.wait()
    load_p.wait()
    half = s_ref.shape[1]
    for part in range(2):
        def st_body(cb, carry, part=part):
            c_at = pl.multiple_of(cb * 128, 128)
            for kb in range(half // 128):
                tile = s_vm[part, kb * 128:(kb + 1) * 128, pl.ds(c_at, 128)].T
                hi, lo = split(tile)
                cols = slice(part * half + kb * 128, part * half + (kb + 1) * 128)
                st_hi[pl.ds(c_at, 128), cols] = hi
                st_lo[pl.ds(c_at, 128), cols] = lo
            return carry

        lax.fori_loop(0, half // 128, st_body, 0)
    weight = jnp.where(ins_ref[0] < sink_ref[0], 1.0, 0.0).astype(F32)
    rows = p_ref.shape[1]
    for spin in range(NSPIN):
        scale = weight if spin < 2 else -weight
        re = p_vm[0, :, spin * nv:(spin + 1) * nv] * scale
        im = p_vm[1, :, spin * nv:(spin + 1) * nv] * scale
        for row, col, val in ((0, 0, re), (0, 1, -im), (1, 0, im), (1, 1, re)):
            hi, lo = split(val)
            p2_hi[spin, row * rows:(row + 1) * rows, col * nv:(col + 1) * nv] = hi
            p2_lo[spin, row * rows:(row + 1) * rows, col * nv:(col + 1) * nv] = lo

    def elemental(z):
        for copy in bra_copies[z]:
            copy.wait_recv()
        for c in range(3):
            re_hi, re_lo = split(bra[z, c])
            im_hi, im_lo = split(bra[z, 3 + c])
            for ref, re, im in ((rhs_hi, re_hi, im_hi), (rhs_lo, re_lo, im_lo)):
                left_cols = slice(c * plane, (c + 1) * plane)
                right_cols = slice((3 + c) * plane, (4 + c) * plane)
                ref[0:nv, left_cols] = re
                ref[0:nv, right_cols] = im
                ref[nv:2 * nv, left_cols] = -im
                ref[nv:2 * nv, right_cols] = re
        part = dot3(ket_hi[z], ket_lo[z], rhs_hi[...], rhs_lo[...], NT).reshape(acc.shape)
        if z == order[0]:
            acc[...] = part
        else:
            acc[...] += part

    for z in order[:-2]:
        elemental(z)

    halo_w.wait()

    def low_body(b, carry):
        above = [own(1, c, b) for c in range(6)]
        z_planes(0, b, above, [halo_dn[c, rows_of(b), :] for c in range(6)])
        return carry

    lax.fori_loop(0, n_block, low_body, 0)
    halo_v.wait()

    def high_body(b, carry):
        above = [halo_up[c, rows_of(b), :] for c in range(6)]
        z_planes(depth - 1, b, above, own_back(depth - 2, b))
        return carry

    lax.fori_loop(0, n_block, high_body, 0)
    for z in order[-2:]:
        elemental(z)

    for m in range(n_mom):
        for e in range(n_dir):
            for part in range(2):
                epart[2 * (m * n_dir + e) + part] = acc[
                    m * n_dir + dir_ref[e], :, part * nv:(part + 1) * nv]

    n_group = pairs2 // n_sp
    per_group = n_sp // 2

    def rs_copy(g, d):
        peer = (me_z + d) % n_sp
        return remote(epart.at[g * n_sp + peer], rs_buf.at[g, d - 1], rs_s.at[g, d - 1],
                      rs_r.at[g, d - 1], "space", peer)

    def ag_copy(g, d):
        return remote(e_own.at[g], e_full.at[g * n_sp + me_z, my_rows, :], ag_s.at[g, d - 1],
                      ag_r.at[g, d - 1], "space", (me_z + d) % n_sp)

    def fx_copy(g, slot, d):
        owner = (me_z + n_sp - slot) % n_sp
        target = e_full.at[g * n_sp + owner, my_rows, :]
        return remote(target if slot else e_own.at[g], target, fx_s.at[g, slot, d - 1],
                      fx_r.at[g, slot, d - 1], "tsink", (me_x + d) % n_ts)

    def reduce(g):
        total = epart[g * n_sp + me_z]
        for d in range(1, n_sp):
            rs_copy(g, d).wait_recv()
            total = total + rs_buf[g, d - 1]
        e_own[g] = total
        e_full[g * n_sp + me_z, my_rows, :] = total
        for d in range(1, n_sp):
            ag_copy(g, d).start()
        for d in range(1, n_ts):
            fx_copy(g, 0, d).start()

    def forward(g):
        for slot in range(1, n_sp):
            ag_copy(g, slot).wait_recv()
            for d in range(1, n_ts):
                fx_copy(g, slot, d).start()

    def left(g):
        for slot in range(n_sp):
            for d in range(1, n_ts):
                fx_copy(g, slot, d).wait_recv()
        for i in range(per_group):
            for part in range(2):
                hi, lo = split(e_full[g * n_sp + 2 * i + part])
                e_hi[i * nv:(i + 1) * nv, part * nv:(part + 1) * nv] = hi
                e_lo[i * nv:(i + 1) * nv, part * nv:(part + 1) * nv] = lo

        def left_body(spin, carry):
            prod = dot3(e_hi[...], e_lo[...], p2_hi[spin], p2_lo[spin], NT)
            at = pl.ds(pl.multiple_of(spin * nv, nv), nv)
            at_low = pl.ds(pl.multiple_of(half + spin * nv, nv), nv)
            for i in range(per_group):
                hi, lo = split(prod[i * nv:(i + 1) * nv])
                for ref, val in ((l2_hi, hi), (l2_lo, lo)):
                    ref[g * per_group + i, at, :] = val
                    ref[g * per_group + i, at_low, 0:rows] = -val[:, rows:]
                    ref[g * per_group + i, at_low, rows:] = val[:, :rows]
            return carry

        lax.fori_loop(0, NSPIN, left_body, 0)

    def spread(g):
        for d in range(1, n_sp):
            rs_copy(g, d).start()

    for g in range(n_group):
        spread(g)
    n_col = recv_a.shape[1]

    def right(q, pair):
        at = pl.ds(pl.multiple_of(pair * (2 * n_col), 2 * n_col), 2 * n_col)
        return dot3(st_hi[at, :], st_lo[at, :], l2_hi[q], l2_lo[q], NN)

    def copy_a(q):
        return remote(tmp_a.at[q, 1 - core], recv_a.at[q], a_s.at[q], a_r.at[q], "tins", mate)

    def copy_y(q):
        return remote(sum_a.at[q], recv_y.at[q], y_s.at[q], y_r.at[q], "tins", far)

    def copy_b(q):
        return remote(tmp_b.at[q, 1 - core], recv_b.at[q], b_s.at[q], b_r.at[q], "tins", mate)

    def relay(q):
        copy_a(q).wait_recv()
        sum_a[q] = tmp_a[q, core] + recv_a[q]
        copy_y(q).start()

    my_pair = me_t // 2

    def near(q):
        res = right(q, 1 - my_pair)
        tmp_a[q, 0] = res[:n_col]
        tmp_a[q, 1] = res[n_col:]
        copy_a(q).start()

    for g in range(n_group + 2):
        if g < n_group:
            reduce(g)
        if 1 <= g <= n_group:
            forward(g - 1)
        if g >= 2:
            left(g - 2)
            for q in range((g - 2) * per_group, (g - 1) * per_group):
                near(q)
                if q:
                    relay(q - 1)
    relay(pairs - 1)
    for q in range(pairs):
        res = right(q, my_pair)
        tmp_b[q, 0] = res[:n_col]
        tmp_b[q, 1] = res[n_col:]
        copy_b(q).start()
    for q in range(pairs):
        copy_b(q).wait_recv()
        copy_y(q).wait_recv()
        val = tmp_b[q, core] + recv_b[q] + recv_y[q]
        for part in range(2):
            out_ref[pl.ds(2 * q + part, n_col, stride=pairs2), :] = (
                val[:, part * rows:(part + 1) * rows])

    for z in order:
        for copy in bra_copies[z]:
            copy.wait_send()
    for g in range(n_group):
        for d in range(1, n_sp):
            rs_copy(g, d).wait_send()
            ag_copy(g, d).wait_send()
        for slot in range(n_sp):
            for d in range(1, n_ts):
                fx_copy(g, slot, d).wait_send()
    for q in range(pairs):
        copy_a(q).wait_send()
        copy_y(q).wait_send()
        copy_b(q).wait_send()


def pair_kernel(
    n_sp, dir_ref, mom_ref, ins_ref, sink_ref, ev_ref, link_hbm, p_ref, s_ref, out_ref,
    link_ref, cos_ref, sin_ref, p_vm, s_vm, in_sem,
    vec_own, vec_far, w_top, halo_up, halo_dn, ket_hi, ket_lo, rhs_own, rhs_far, acc_own, acc_far,
    part_own, part_far, buf_own, buf_far, sum_own, sum_far, e_full, e_two, st_two,
    p2_hi, p2_lo, l2_hi, l2_lo, tmp_a, recv_a, sum_a, tmp_b, recv_b, recv_y,
    loc_sem, v_s, v_r, halo_s, halo_r, rd_s, rd_r, gd_s, gd_r, xd_s, xd_r,
    rf_s, rf_r, gf_s, gf_r, xf_s, xf_r, a_s, a_r, y_s, y_r, b_s, b_r,
):
    _, vecs, depth, plane = ev_ref.shape
    pairs = part_own.shape[1]
    n_dir = 3
    n_mom = pairs // n_dir
    nv = 2 * vecs
    me_x = lax.axis_index("tsink")
    me_z = lax.axis_index("space")
    me_t = lax.axis_index("tins")
    core = me_t % 2
    mate = me_t + 1 - 2 * core
    far = (me_t + 2) % 4
    up = (me_z + 1) % n_sp
    down = (me_z + n_sp - 1) % n_sp
    other = 1 - me_x
    is_head = me_x == core
    not_head = me_x != core

    barrier = pltpu.get_barrier_semaphore()
    mesh_type = pl.DeviceIdType.MESH
    pl.semaphore_signal(barrier, inc=1, device_id={"tsink": other}, device_id_type=mesh_type)
    for d in range(1, n_sp):
        pl.semaphore_signal(barrier, inc=1, device_id={"space": (me_z + d) % n_sp},
                            device_id_type=mesh_type)
    for target in (mate, far):
        pl.semaphore_signal(barrier, inc=1, device_id={"tins": target}, device_id_type=mesh_type)
    local = [
        pltpu.make_async_copy(ev_ref.at[:, :, z, :], vec_own.at[z], loc_sem.at[z])
        for z in range(depth)
    ]
    local[depth - 1].start()
    load_links = pltpu.make_async_copy(link_hbm, link_ref, in_sem.at[2])
    load_links.start()
    for copy in local[:-1]:
        copy.start()
    load_p = pltpu.make_async_copy(p_ref, p_vm, in_sem.at[0])
    load_s = pltpu.make_async_copy(s_ref, s_vm, in_sem.at[1])
    load_p.start()
    load_s.start()
    order = list(range(1, depth - 1)) + [0, depth - 1]
    vec_copies = {
        z: remote(ev_ref.at[:, :, z, :], vec_far.at[z], v_s.at[z], v_r.at[z], "tsink", other)
        for z in order
    }
    halo_v = remote(ev_ref.at[:, :, 0, :], halo_up, halo_s.at[0], halo_r.at[0], "space", down)
    halo_w = remote(w_top, halo_dn, halo_s.at[1], halo_r.at[1], "space", up)

    block = min(16, vecs)
    n_block = vecs // block

    def rows_of(b):
        return pl.ds(pl.multiple_of(b * block, block), block)

    def own(z, c, b):
        return vec_own[z, c, rows_of(b), :]

    def links_at(k, z):
        return [
            [[link_ref[k, part, i, j, pl.ds(z, 1), :] for j in range(3)] for i in range(3)]
            for part in range(2)
        ]

    column = lax.broadcasted_iota(jnp.int32, (block, plane), 1) % L

    def shifted(x, k, sign):
        if k == 1:
            return pltpu.roll(x, plane - L if sign > 0 else L, axis=1)
        if sign > 0:
            return jnp.where(column == L - 1, pltpu.roll(x, L - 1, axis=1),
                             pltpu.roll(x, plane - 1, axis=1))
        return jnp.where(column == 0, pltpu.roll(x, plane + 1 - L, axis=1),
                         pltpu.roll(x, 1, axis=1))

    site = lax.broadcasted_iota(jnp.int32, (depth, plane), 1)
    z_coord = me_z * depth + lax.broadcasted_iota(jnp.int32, (depth, plane), 0)
    for m in range(n_mom):
        product = mom_ref[m, 0] * (site % L) + mom_ref[m, 1] * (site // L) + mom_ref[m, 2] * z_coord
        steps = [0] + [mom_ref[m, k] for k in range(n_dir)] + [-mom_ref[m, k] for k in range(n_dir)]
        for j, step in enumerate(steps):
            angles = (2.0 * math.pi / L) * jnp.bitwise_and(product + step, L - 1).astype(F32)
            cos_ref[m, j] = jnp.cos(angles)
            sin_ref[m, j] = jnp.sin(angles)

    def put_kets(k, z, b, ahead, back, turned):
        deriv = [ahead[c] - back[c] for c in range(6)]

        def put(start, i, re, im):
            at = pl.multiple_of(start * vecs + b * block, block)
            for comp, val in ((i, re), (3 + i, im)):
                hi, lo = split(val)
                cols = slice(comp * plane, (comp + 1) * plane)
                ket_hi[z, pl.ds(at, block), cols] = hi
                ket_lo[z, pl.ds(at, block), cols] = lo

        for m in range(n_mom):
            c, c_up, c_dn = [cos_ref[m, j, pl.ds(z, 1), :] for j in (0, 1 + k, 1 + n_dir + k)]
            s, s_up, s_dn = [sin_ref[m, j, pl.ds(z, 1), :] for j in (0, 1 + k, 1 + n_dir + k)]
            for i in range(3):
                put(m * n_dir + k, i, c * deriv[i] + s * deriv[3 + i],
                    c * deriv[3 + i] - s * deriv[i])
                if not turned:
                    continue
                re = c_up * ahead[i] - s_up * ahead[3 + i]
                im = c_up * ahead[3 + i] + s_up * ahead[i]
                if turned == 2:
                    re = re - c_dn * back[i] + s_dn * back[3 + i]
                    im = im - c_dn * back[3 + i] - s_dn * back[i]
                put(pairs + m * n_dir + k, i, re, im)

    def by_role(count, body, head_turned, turned):
        @pl.when(is_head)
        def _():
            lax.fori_loop(0, count, functools.partial(body, head_turned), 0)

        @pl.when(not_head)
        def _():
            lax.fori_loop(0, count, functools.partial(body, turned), 0)

    pl.semaphore_wait(barrier, 1 + n_sp - 1 + 2)

    @pl.when(is_head)
    def _():
        halo_v.start()

    @pl.when(not_head)
    def _():
        for z in order:
            vec_copies[z].start()
        halo_dn[...] = jnp.zeros_like(halo_dn)

    load_links.wait()
    local[depth - 1].wait()

    def top_body(b, carry):
        vec = [own(depth - 1, c, b) for c in range(6)]
        w = colour_rows(links_at(2, depth - 1), vec, True)
        for c in range(6):
            w_top[c, rows_of(b), :] = w[c]
        return carry

    @pl.when(is_head)
    def _():
        lax.fori_loop(0, n_block, top_body, 0)
        halo_w.start()

    @pl.when(not_head)
    def _():
        halo_v.start()

    for copy in local[:-1]:
        copy.wait()

    for k in range(2):
        def xy_body(turned, t, carry, k=k):
            z = t // n_block
            b = t % n_block
            vec = [own(z, c, b) for c in range(6)]
            link = links_at(k, z)
            ahead = colour_rows(link, [shifted(x, k, 1) for x in vec], False)
            back = colour_rows(link, vec, True)
            put_kets(k, z, b, ahead, [shifted(x, k, -1) for x in back], turned)
            return carry

        by_role(depth * n_block, xy_body, 2, 0)

    def z_planes(z, b, above, below, turned):
        put_kets(2, z, b, colour_rows(links_at(2, z), above, False), below, turned)

    def own_back(z, b):
        return colour_rows(links_at(2, z), [own(z, c, b) for c in range(6)], True)

    def mid_body(turned, t, carry):
        z = t // n_block + 1
        b = t % n_block
        z_planes(z, b, [own(z + 1, c, b) for c in range(6)], own_back(z - 1, b),
                 turned)
        return carry

    by_role((depth - 2) * n_block, mid_body, 2, 0)

    def fill(rhs, vec, z):
        for c in range(3):
            left_cols = slice(c * plane, (c + 1) * plane)
            right_cols = slice((3 + c) * plane, (4 + c) * plane)
            for at, re, im in zip((0, nv), split(vec[z, c]), split(vec[z, 3 + c])):
                rhs[at:at + vecs, left_cols] = re
                rhs[at:at + vecs, right_cols] = im
                rhs[at + vecs:at + nv, left_cols] = -im
                rhs[at + vecs:at + nv, right_cols] = re

    def elemental(z, rhs, acc, start):
        rows = pairs * vecs
        both = lax.dot_general(ket_hi[z, start:start + rows, :], rhs[...], NT,
                               preferred_element_type=F32)
        low = lax.dot_general(ket_lo[z, start:start + rows, :], rhs[0:nv, :], NT,
                              preferred_element_type=F32)
        part = (both[:, :nv] + both[:, nv:] + low).reshape(pairs, vecs, nv)
        at = slice(start // vecs, start // vecs + pairs)
        if z == order[0]:
            acc[at] = part
        else:
            acc[at] += part

    def own_elemental(z):
        fill(rhs_own, vec_own, z)
        elemental(z, rhs_own, acc_own, 0)

    def far_elemental(z):
        @pl.when(is_head)
        def _():
            vec_copies[z].wait_recv()
            fill(rhs_far, vec_far, z)
            for start in (0, pairs * vecs):
                elemental(z, rhs_far, acc_far, start)

    for z in order[:-2]:
        own_elemental(z)

    load_s.wait()
    load_p.wait()
    half = s_ref.shape[1]
    wide = half // 2
    for part in range(2):
        def st_body(cb, carry, part=part):
            c_at = pl.multiple_of(cb * 128, 128)
            for kb in range(half // nv):
                near_at = pl.multiple_of(kb * nv + core * vecs, vecs)
                far_at = pl.multiple_of(kb * nv + (1 - core) * vecs, vecs)
                tile = jnp.concatenate([s_vm[part, pl.ds(near_at, vecs), pl.ds(c_at, 128)],
                                        s_vm[part, pl.ds(far_at, vecs), pl.ds(c_at, 128)]], axis=0).T
                hi, lo = split(tile)
                cols = slice(part * half + kb * nv, part * half + (kb + 1) * nv)
                at = pl.multiple_of(cb // 2 * (2 * wide) + cb % 2 * 128, 128)
                st_two[pl.ds(at, 128), cols] = hi
                st_two[pl.ds(at + wide, 128), cols] = lo
            return carry

        lax.fori_loop(0, half // 128, st_body, 0)
    weight = jnp.where(ins_ref[0] < sink_ref[0], 1.0, 0.0).astype(F32)
    rows = p_ref.shape[1]
    low_lane = lax.broadcasted_iota(jnp.int32, (rows, nv), 1) < vecs
    for spin in range(NSPIN):
        scale = weight if spin < 2 else -weight
        re = p_vm[0, :, spin * nv:(spin + 1) * nv] * scale
        im = p_vm[1, :, spin * nv:(spin + 1) * nv] * scale
        re_roll = pltpu.roll(re, vecs, axis=1)
        im_roll = pltpu.roll(im, vecs, axis=1)
        re, re_roll = jnp.where(core == 0, re, re_roll), jnp.where(core == 0, re_roll, re)
        im, im_roll = jnp.where(core == 0, im, im_roll), jnp.where(core == 0, im_roll, im)
        for row, (x, x_roll, y, y_roll) in enumerate(((re, re_roll, -im, -im_roll),
                                                      (im, im_roll, re, re_roll))):
            for col, val in enumerate((jnp.where(low_lane, x, y_roll), jnp.where(low_lane, x_roll, y))):
                hi, lo = split(val)
                p2_hi[spin, row * rows:(row + 1) * rows, col * nv:(col + 1) * nv] = hi
                p2_lo[spin, row * rows:(row + 1) * rows, col * nv:(col + 1) * nv] = lo

    far_elemental(order[0])
    halo_v.wait()

    def high_body(turned, b, carry):
        above = [halo_up[c, rows_of(b), :] for c in range(6)]
        z_planes(depth - 1, b, above, own_back(depth - 2, b), turned)
        return carry

    by_role(n_block, high_body, 2, 1)
    own_elemental(depth - 1)

    def turn(val):
        flat = val.T
        return jnp.concatenate([-flat[:vecs], flat[vecs:]], axis=1)

    @pl.when(not_head)
    def _():
        for m in range(n_mom):
            q = m * n_dir + n_dir - 1
            at = slice((pairs + q) * vecs, (pairs + q + 1) * vecs)
            both = lax.dot_general(ket_hi[depth - 1, at, :], rhs_own[...], NT,
                                   preferred_element_type=F32)
            low = lax.dot_general(ket_lo[depth - 1, at, :], rhs_own[0:nv, :], NT,
                                  preferred_element_type=F32)
            acc_own[q] += turn(both[:, :nv] + both[:, nv:] + low)

    @pl.when(is_head)
    def _():
        halo_w.wait()

    def low_body(turned, b, carry):
        above = [own(1, c, b) for c in range(6)]
        z_planes(0, b, above, [halo_dn[c, rows_of(b), :] for c in range(6)], turned)
        return carry

    by_role(n_block, low_body, 2, 0)
    own_elemental(0)

    strip = vecs // n_sp
    per_group = part_far.shape[2]
    n_group = pairs // per_group
    my_strip = pl.ds(pl.multiple_of(me_z * strip, strip), strip)
    corner = jnp.where(is_head, 0, 3)

    def chosen(acc, q, base):
        return acc[base + (q // n_dir) * n_dir + dir_ref[q % n_dir]]

    def strips(val):
        return [val[z * strip:(z + 1) * strip, :] for z in range(n_sp)]

    for q in range(pairs):
        for z, val in enumerate(strips(chosen(acc_own, q, 0))):
            part_own[z, q] = val

    def rd_copy(d):
        peer = (me_z + d) % n_sp
        return remote(part_own.at[peer], buf_own.at[d - 1], rd_s.at[d - 1], rd_r.at[d - 1],
                      "space", peer)

    def gd_copy(d):
        return remote(sum_own, e_full.at[:, corner, my_strip, :], gd_s.at[d - 1], gd_r.at[d - 1],
                      "space", (me_z + d) % n_sp)

    def xd_copy(g):
        block_at = e_full.at[pl.ds(g * per_group, per_group), corner]
        return remote(block_at, block_at, xd_s.at[g], xd_r.at[g], "tsink", other)

    def rf_copy(g, d):
        peer = (me_z + d) % n_sp
        return remote(part_far.at[g, peer], buf_far.at[g, d - 1], rf_s.at[g, d - 1],
                      rf_r.at[g, d - 1], "space", peer)

    def mixed(g, strip_at):
        return e_full.at[pl.ds(g * per_group, per_group), pl.ds(1, 2), strip_at, :]

    def gf_copy(g, d):
        return remote(sum_far.at[g], mixed(g, my_strip), gf_s.at[g, d - 1], gf_r.at[g, d - 1],
                      "space", (me_z + d) % n_sp)

    def xf_copy(g, slot):
        return pltpu.make_async_remote_copy(
            src_ref=sum_far.at[g], dst_ref=mixed(g, my_strip), send_sem=xf_s.at[g, slot],
            recv_sem=xf_r.at[g, slot], device_id={"tsink": other, "space": (me_z + slot) % n_sp},
            device_id_type=pl.DeviceIdType.MESH)

    for d in range(1, n_sp):
        rd_copy(d).start()
    for z in order[1:-1]:
        far_elemental(z)
    total = part_own[me_z]
    for d in range(1, n_sp):
        rd_copy(d).wait_recv()
        total = total + buf_own[d - 1]
    sum_own[...] = total
    e_full[:, corner, my_strip, :] = total
    for d in range(1, n_sp):
        gd_copy(d).start()
    far_elemental(order[-1])

    @pl.when(is_head)
    def _():
        for q in range(pairs):
            g, i = q // per_group, q % per_group
            for z, val in enumerate(strips(chosen(acc_far, q, 0))):
                part_far[g, z, i, 0] = val
            for z, val in enumerate(strips(turn(chosen(acc_far, q, pairs)))):
                part_far[g, z, i, 1] = val
            if i == per_group - 1:
                for d in range(1, n_sp):
                    rf_copy(g, d).start()

    @pl.when(not_head)
    def _():
        for z in order:
            vec_copies[z].wait_send()

    def reduce(g):
        @pl.when(is_head)
        def _():
            total = part_far[g, me_z]
            for d in range(1, n_sp):
                rf_copy(g, d).wait_recv()
                total = total + buf_far[g, d - 1]
            sum_far[g] = total
            e_full[pl.ds(g * per_group, per_group), pl.ds(1, 2), my_strip, :] = total
            for d in range(1, n_sp):
                gf_copy(g, d).start()
            for slot in range(n_sp):
                xf_copy(g, slot).start()

    def forward(g):
        @pl.when(is_head)
        def _():
            for d in range(1, n_sp):
                gf_copy(g, d).wait_recv()

    def left(g):
        xd_copy(g).wait_recv()

        @pl.when(not_head)
        def _():
            for slot in range(n_sp):
                xf_copy(g, slot).wait_recv()

        for i in range(per_group):
            for quad in range(4):
                hi, lo = split(e_full[g * per_group + i, quad])
                at = i * nv + quad // 2 * vecs
                low_at = at + per_group * nv
                cols = slice(quad % 2 * nv, (quad % 2 + 1) * nv)
                e_two[at:at + vecs, cols] = hi
                e_two[low_at:low_at + vecs, cols] = lo

        def left_body(spin, carry):
            prod = dot_two(e_two[...], p2_hi[spin], p2_lo[spin], NT)
            at = pl.ds(pl.multiple_of(spin * nv, nv), nv)
            at_low = pl.ds(pl.multiple_of(half + spin * nv, nv), nv)
            for i in range(per_group):
                hi, lo = split(prod[i * nv:(i + 1) * nv])
                for ref, val in ((l2_hi, hi), (l2_lo, lo)):
                    ref[g * per_group + i, at, :] = val
                    ref[g * per_group + i, at_low, 0:rows] = -val[:, rows:]
                    ref[g * per_group + i, at_low, rows:] = val[:, :rows]
            return carry

        lax.fori_loop(0, NSPIN, left_body, 0)

    n_col = recv_a.shape[1]

    def right(q, pair):
        at = pl.ds(pl.multiple_of(pair * (2 * wide), 2 * wide), 2 * wide)
        return dot_two(st_two[at, :], l2_hi[q], l2_lo[q], NN)

    def copy_a(q):
        return remote(tmp_a.at[q, 1 - core], recv_a.at[q], a_s.at[q], a_r.at[q], "tins", mate)

    def copy_y(q):
        return remote(sum_a.at[q], recv_y.at[q], y_s.at[q], y_r.at[q], "tins", far)

    def copy_b(q):
        return remote(tmp_b.at[q, 1 - core], recv_b.at[q], b_s.at[q], b_r.at[q], "tins", mate)

    def relay(q):
        copy_a(q).wait_recv()
        sum_a[q] = tmp_a[q, core] + recv_a[q]
        copy_y(q).start()

    my_pair = me_t // 2

    def near(q):
        res = right(q, 1 - my_pair)
        tmp_a[q, 0] = res[:n_col]
        tmp_a[q, 1] = res[n_col:]
        copy_a(q).start()

    ahead = min(2, n_group)

    def spread_own():
        for d in range(1, n_sp):
            gd_copy(d).wait_recv()
        for h in range(n_group):
            xd_copy(h).start()

    for g in range(ahead):
        if g == 1:
            spread_own()
        reduce(g)
    for g in range(n_group):
        if g + ahead < n_group:
            reduce(g + ahead)
        forward(g)
        left(g)
        for q in range(g * per_group, (g + 1) * per_group):
            if q:
                relay(q - 1)
            near(q)
    for q in range(pairs):
        res = right(q, my_pair)
        if q == 0:
            relay(pairs - 1)
        tmp_b[q, 0] = res[:n_col]
        tmp_b[q, 1] = res[n_col:]
        copy_b(q).start()
    for q in range(pairs):
        copy_b(q).wait_recv()
        copy_y(q).wait_recv()
        val = tmp_b[q, core] + recv_b[q] + recv_y[q]
        for part in range(2):
            out_ref[pl.ds(2 * q + part, n_col, stride=2 * pairs), :] = (
                val[:, part * rows:(part + 1) * rows])

    for d in range(1, n_sp):
        rd_copy(d).wait_send()
        gd_copy(d).wait_send()

    @pl.when(is_head)
    def _():
        for g in range(n_group):
            for d in range(1, n_sp):
                rf_copy(g, d).wait_send()
                gf_copy(g, d).wait_send()
            for slot in range(n_sp):
                xf_copy(g, slot).wait_send()

    for g in range(n_group):
        xd_copy(g).wait_send()
    for q in range(pairs):
        copy_a(q).wait_send()
        copy_y(q).wait_send()
        copy_b(q).wait_send()


def copy_kernel(in_ref, out_ref):
    out_ref[...] = in_ref[...]


def ring_call(n_ts, n_sp, n_ti, eigvecs, links, momenta, directions, ins_time, sink_time,
              sink_peramb, source_peramb):
    assert n_ti == 4
    _, _, _, vecs, depth, plane = eigvecs.shape
    nv = vecs * n_ts
    ev = eigvecs.reshape(6, vecs, depth, plane)
    pairs = momenta.shape[0] * directions.shape[0]
    order_m = source_peramb.shape[-1]
    rows = sink_peramb.shape[3]
    n_col = order_m // n_ti
    n_group = 2 * pairs // n_sp
    v = pltpu.VMEM
    dma = pltpu.SemaphoreType.DMA
    scratch = [
        v((momenta.shape[0], depth, plane), F32), v((momenta.shape[0], depth, plane), F32),
        v(sink_peramb.shape[2:], F32), v(source_peramb.shape[1:], F32), dma((2,)),
        v((depth, 6, nv, plane), F32),
        v((6, vecs, plane), F32), v((6, vecs, plane), F32), v((6, vecs, plane), F32),
        v((depth, pairs * vecs, 6 * plane), BF16), v((depth, pairs * vecs, 6 * plane), BF16),
        v((2 * nv, 6 * plane), BF16), v((2 * nv, 6 * plane), BF16),
        v((pairs, vecs, 2 * nv), F32),
        v((2 * pairs, vecs, nv), F32),
        v((n_group, n_sp - 1, vecs, nv), F32),
        v((n_group, vecs, nv), F32),
        v((2 * pairs, nv, nv), F32),
        v((n_sp // 2 * nv, 2 * nv), BF16), v((n_sp // 2 * nv, 2 * nv), BF16),
        v((order_m, 2 * order_m), BF16), v((order_m, 2 * order_m), BF16),
        v((NSPIN, 2 * rows, 2 * nv), BF16), v((NSPIN, 2 * rows, 2 * nv), BF16),
        v((pairs, 2 * order_m, 2 * rows), BF16), v((pairs, 2 * order_m, 2 * rows), BF16),
        v((pairs, 2, n_col, 2 * rows), F32),
        v((pairs, n_col, 2 * rows), F32), v((pairs, n_col, 2 * rows), F32),
        v((pairs, 2, n_col, 2 * rows), F32),
        v((pairs, n_col, 2 * rows), F32), v((pairs, n_col, 2 * rows), F32),
        dma((depth,)), dma((depth, n_ts - 1)), dma((depth, n_ts - 1)), dma((2,)), dma((2,)),
        dma((n_group, n_sp - 1)), dma((n_group, n_sp - 1)),
        dma((n_group, n_sp - 1)), dma((n_group, n_sp - 1)),
        dma((n_group, n_sp, n_ts - 1)), dma((n_group, n_sp, n_ts - 1)),
        dma((pairs,)), dma((pairs,)), dma((pairs,)), dma((pairs,)), dma((pairs,)), dma((pairs,)),
    ]
    smem = pl.BlockSpec(memory_space=pltpu.SMEM)
    vmem = pl.BlockSpec(memory_space=pltpu.VMEM)
    hbm = pl.BlockSpec(memory_space=pl.ANY)
    out = pl.pallas_call(
        functools.partial(ring_kernel, n_ts, n_sp),
        out_shape=jax.ShapeDtypeStruct((n_col * pairs * 2, rows), F32),
        in_specs=[smem] * 4 + [hbm, vmem, hbm, hbm],
        out_specs=vmem,
        scratch_shapes=scratch,
        compiler_params=pltpu.CompilerParams(
            collective_id=0, has_side_effects=True, vmem_limit_bytes=60 * 1024 * 1024
        ),
        name="peramb",
    )(directions, momenta, ins_time, sink_time, ev, links[0], sink_peramb[0, 0],
      source_peramb[0])
    tile = pl.BlockSpec((out.shape[0] // 2, rows), lambda i: (i, 0))
    out = pl.pallas_call(
        copy_kernel,
        grid=(2,),
        out_shape=jax.ShapeDtypeStruct(out.shape, F32),
        in_specs=[tile],
        out_specs=tile,
        name="result",
    )(out)
    return out.reshape(n_col, 1, pairs, 2, rows)


def pair_call(n_ts, n_sp, n_ti, eigvecs, links, momenta, directions, ins_time, sink_time,
              sink_peramb, source_peramb):
    assert n_ts == 2 and n_ti == 4
    _, _, _, vecs, depth, plane = eigvecs.shape
    nv = vecs * n_ts
    ev = eigvecs.reshape(6, vecs, depth, plane)
    n_mom = momenta.shape[0]
    pairs = n_mom * directions.shape[0]
    order_m = source_peramb.shape[-1]
    rows = sink_peramb.shape[3]
    n_col = order_m // n_ti
    per_group = 1
    n_group = pairs // per_group
    strip = vecs // n_sp
    v = pltpu.VMEM
    dma = pltpu.SemaphoreType.DMA
    scratch = [
        v(links.shape[1:], F32), v((n_mom, 7, depth, plane), F32), v((n_mom, 7, depth, plane), F32),
        v(sink_peramb.shape[2:], F32), v(source_peramb.shape[1:], F32), dma((3,)),
        v((depth, 6, vecs, plane), F32), v((depth, 6, vecs, plane), F32),
        v((6, vecs, plane), F32), v((6, vecs, plane), F32), v((6, vecs, plane), F32),
        v((depth, 2 * pairs * vecs, 6 * plane), BF16), v((depth, 2 * pairs * vecs, 6 * plane), BF16),
        v((2 * nv, 6 * plane), BF16), v((2 * nv, 6 * plane), BF16),
        v((pairs, vecs, nv), F32), v((2 * pairs, vecs, nv), F32),
        v((n_sp, pairs, strip, nv), F32), v((n_group, n_sp, per_group, 2, strip, nv), F32),
        v((n_sp - 1, pairs, strip, nv), F32), v((n_group, n_sp - 1, per_group, 2, strip, nv), F32),
        v((pairs, strip, nv), F32), v((n_group, per_group, 2, strip, nv), F32),
        v((pairs, 4, vecs, nv), F32),
        v((2 * per_group * nv, 2 * nv), BF16), v((2 * order_m, 2 * order_m), BF16),
        v((NSPIN, 2 * rows, 2 * nv), BF16), v((NSPIN, 2 * rows, 2 * nv), BF16),
        v((pairs, 2 * order_m, 2 * rows), BF16), v((pairs, 2 * order_m, 2 * rows), BF16),
        v((pairs, 2, n_col, 2 * rows), F32),
        v((pairs, n_col, 2 * rows), F32), v((pairs, n_col, 2 * rows), F32),
        v((pairs, 2, n_col, 2 * rows), F32),
        v((pairs, n_col, 2 * rows), F32), v((pairs, n_col, 2 * rows), F32),
        dma((depth,)), dma((depth,)), dma((depth,)), dma((2,)), dma((2,)),
        dma((n_sp - 1,)), dma((n_sp - 1,)), dma((n_sp - 1,)), dma((n_sp - 1,)),
        dma((n_group,)), dma((n_group,)),
        dma((n_group, n_sp - 1)), dma((n_group, n_sp - 1)),
        dma((n_group, n_sp - 1)), dma((n_group, n_sp - 1)),
        dma((n_group, n_sp)), dma((n_group, n_sp)),
        dma((pairs,)), dma((pairs,)), dma((pairs,)), dma((pairs,)), dma((pairs,)), dma((pairs,)),
    ]
    smem = pl.BlockSpec(memory_space=pltpu.SMEM)
    vmem = pl.BlockSpec(memory_space=pltpu.VMEM)
    hbm = pl.BlockSpec(memory_space=pl.ANY)
    out = pl.pallas_call(
        functools.partial(pair_kernel, n_sp),
        out_shape=jax.ShapeDtypeStruct((n_col * pairs * 2, rows), F32),
        in_specs=[smem] * 4 + [hbm] * 4,
        out_specs=vmem,
        scratch_shapes=scratch,
        compiler_params=pltpu.CompilerParams(
            collective_id=0, has_side_effects=True, vmem_limit_bytes=60 * 1024 * 1024
        ),
        name="peramb",
    )(directions, momenta, ins_time, sink_time, ev, links[0], sink_peramb[0, 0],
      source_peramb[0])
    tile = pl.BlockSpec((out.shape[0] // 2, rows), lambda i: (i, 0))
    out = pl.pallas_call(
        copy_kernel,
        grid=(2,),
        out_shape=jax.ShapeDtypeStruct(out.shape, F32),
        in_specs=[tile],
        out_specs=tile,
        name="result",
    )(out)
    return out.reshape(n_col, 1, pairs, 2, rows)


def solution(mesh):
    in_specs = (
        P("tins", None, None, "tsink", "space", None),
        P("tins", None, None, None, None, "space", None),
        P(),
        P(),
        P("tins"),
        P("tsink"),
        P("tsink", "tins", None, "space", None),
        P("tins", None, None, None),
    )
    out_specs = P("tins", "tsink", None, None, "space")
    sizes = mesh.shape["tsink"], mesh.shape["space"], mesh.shape["tins"]
    body = functools.partial(pair_call if sizes[0] == 2 else ring_call, *sizes)
    return jax.shard_map(body, mesh=mesh, in_specs=in_specs, out_specs=out_specs, check_vma=False)
```

```python
import functools
import math

import jax
import jax.numpy as jnp
from jax import lax
from jax.experimental import pallas as pl
from jax.experimental.pallas import tpu as pltpu
from jax.sharding import PartitionSpec as P

L = 16
NSPIN = 4
BF16 = jnp.bfloat16
F32 = jnp.float32
NT = (((1,), (1,)), ((), ()))
NN = (((1,), (0,)), ((), ()))


def split(x):
    hi = x.astype(BF16)
    return hi, (x - hi.astype(F32)).astype(BF16)


def dot3(a_hi, a_lo, b_hi, b_lo, dims):
    def one(a, b):
        return lax.dot_general(a, b, dims, preferred_element_type=F32)

    return one(a_hi, b_hi) + one(a_hi, b_lo) + one(a_lo, b_hi)


def dot_two(a, b_hi, b_lo, dims):
    rows = a.shape[0] // 2
    both = lax.dot_general(a, b_hi, dims, preferred_element_type=F32)
    low = lax.dot_general(a[:rows], b_lo, dims, preferred_element_type=F32)
    return both[:rows] + both[rows:] + low


def remote(src, dst, send, recv, axis, index):
    return pltpu.make_async_remote_copy(
        src_ref=src,
        dst_ref=dst,
        send_sem=send,
        recv_sem=recv,
        device_id={axis: index},
        device_id_type=pl.DeviceIdType.MESH,
    )


def colour_rows(link, vec, adjoint):
    rows = []
    for i in range(3):
        re = im = None
        for j in range(3):
            if adjoint:
                a, b = link[0][j][i], link[1][j][i]
                tr = a * vec[j] + b * vec[3 + j]
                ti = a * vec[3 + j] - b * vec[j]
            else:
                a, b = link[0][i][j], link[1][i][j]
                tr = a * vec[j] - b * vec[3 + j]
                ti = a * vec[3 + j] + b * vec[j]
            re = tr if re is None else re + tr
            im = ti if im is None else im + ti
        rows.append((re, im))
    return [r[0] for r in rows] + [r[1] for r in rows]


def ring_kernel(
    n_ts, n_sp, dir_ref, mom_ref, ins_ref, sink_ref, ev_ref, link_ref, p_ref, s_ref, out_ref,
    cos_ref, sin_ref, p_vm, s_vm, in_sem,
    bra, w_top, halo_up, halo_dn, ket_hi, ket_lo, rhs_hi, rhs_lo, acc, epart, rs_buf, e_own,
    e_full, e_hi, e_lo, st_hi, st_lo, p2_hi, p2_lo, l2_hi, l2_lo, tmp_a, recv_a, sum_a, tmp_b,
    recv_b, recv_y, loc_sem, bra_s, bra_r, halo_s, halo_r, rs_s, rs_r, ag_s, ag_r, fx_s, fx_r,
    a_s, a_r, y_s, y_r, b_s, b_r,
):
    _, vecs, depth, plane = ev_ref.shape
    pairs2 = epart.shape[0]
    pairs = pairs2 // 2
    n_dir = 3
    n_mom = pairs // n_dir
    nv = bra.shape[2]
    me_x = lax.axis_index("tsink")
    me_z = lax.axis_index("space")
    me_t = lax.axis_index("tins")
    core = me_t % 2
    mate = me_t + 1 - 2 * core
    far = (me_t + 2) % 4
    up = (me_z + 1) % n_sp
    down = (me_z + n_sp - 1) % n_sp
    my_rows = pl.ds(pl.multiple_of(me_x * vecs, vecs), vecs)
    local = [
        pltpu.make_async_copy(ev_ref.at[:, :, z, :], bra.at[z, :, my_rows, :], loc_sem.at[z])
        for z in range(depth)
    ]
    for copy in reversed(local):
        copy.start()
    load_p = pltpu.make_async_copy(p_ref, p_vm, in_sem.at[0])
    load_s = pltpu.make_async_copy(s_ref, s_vm, in_sem.at[1])
    load_p.start()
    load_s.start()
    barrier = pltpu.get_barrier_semaphore()
    mesh_type = pl.DeviceIdType.MESH
    for d in range(1, n_ts):
        pl.semaphore_signal(barrier, inc=1, device_id={"tsink": (me_x + d) % n_ts},
                            device_id_type=mesh_type)
    for d in range(1, n_sp):
        pl.semaphore_signal(barrier, inc=1, device_id={"space": (me_z + d) % n_sp},
                            device_id_type=mesh_type)
    for target in (mate, far):
        pl.semaphore_signal(barrier, inc=1, device_id={"tins": target}, device_id_type=mesh_type)
    pl.semaphore_wait(barrier, n_ts - 1 + n_sp - 1 + 2)

    order = list(range(1, depth - 1)) + [0, depth - 1]
    bra_copies = {}
    for z in order:
        bra_copies[z] = [
            remote(ev_ref.at[:, :, z, :], bra.at[z, :, my_rows, :], bra_s.at[z, d - 1], bra_r.at[z, d - 1],
                   "tsink", (me_x + d) % n_ts)
            for d in range(1, n_ts)
        ]
    halo_v = remote(ev_ref.at[:, :, 0, :], halo_up, halo_s.at[0], halo_r.at[0], "space", down)
    halo_w = remote(w_top, halo_dn, halo_s.at[1], halo_r.at[1], "space", up)
    halo_v.start()
    for z in order:
        for copy in bra_copies[z]:
            copy.start()

    block = min(16, vecs)
    n_block = vecs // block

    def rows_of(b):
        return pl.ds(pl.multiple_of(b * block, block), block)

    def own(z, c, b):
        return bra[z, c, pl.ds(pl.multiple_of(me_x * vecs + b * block, block), block), :]

    def links_at(k, z):
        return [
            [[link_ref[k, part, i, j, pl.ds(z, 1), :] for j in range(3)] for i in range(3)]
            for part in range(2)
        ]

    column = lax.broadcasted_iota(jnp.int32, (block, plane), 1) % L

    def shifted(x, k, sign):
        if k == 1:
            return pltpu.roll(x, plane - L if sign > 0 else L, axis=1)
        if sign > 0:
            return jnp.where(column == L - 1, pltpu.roll(x, L - 1, axis=1),
                             pltpu.roll(x, plane - 1, axis=1))
        return jnp.where(column == 0, pltpu.roll(x, plane + 1 - L, axis=1),
                         pltpu.roll(x, 1, axis=1))

    site = lax.broadcasted_iota(jnp.int32, (depth, plane), 1)
    z_coord = me_z * depth + lax.broadcasted_iota(jnp.int32, (depth, plane), 0)
    for m in range(n_mom):
        product = mom_ref[m, 0] * (site % L) + mom_ref[m, 1] * (site // L) + mom_ref[m, 2] * z_coord
        angles = (2.0 * math.pi / L) * jnp.bitwise_and(product, L - 1).astype(F32)
        cos_ref[m] = jnp.cos(angles)
        sin_ref[m] = jnp.sin(angles)

    def put_kets(k, z, b, deriv):
        for m in range(n_mom):
            c = cos_ref[m, pl.ds(z, 1), :]
            s = sin_ref[m, pl.ds(z, 1), :]
            start = pl.multiple_of((m * n_dir + k) * vecs + b * block, block)
            for i in range(3):
                for comp, val in (
                    (i, c * deriv[i] + s * deriv[3 + i]),
                    (3 + i, c * deriv[3 + i] - s * deriv[i]),
                ):
                    hi, lo = split(val)
                    cols = slice(comp * plane, (comp + 1) * plane)
                    ket_hi[z, pl.ds(start, block), cols] = hi
                    ket_lo[z, pl.ds(start, block), cols] = lo

    local[depth - 1].wait()

    def top_body(b, carry):
        vec = [own(depth - 1, c, b) for c in range(6)]
        w = colour_rows(links_at(2, depth - 1), vec, True)
        for c in range(6):
            w_top[c, rows_of(b), :] = w[c]
        return carry

    lax.fori_loop(0, n_block, top_body, 0)
    halo_w.start()
    for copy in local[:-1]:
        copy.wait()

    for k in range(2):
        def xy_body(t, carry, k=k):
            z = t // n_block
            b = t % n_block
            vec = [own(z, c, b) for c in range(6)]
            link = links_at(k, z)
            ahead = colour_rows(link, [shifted(x, k, 1) for x in vec], False)
            back = colour_rows(link, vec, True)
            put_kets(k, z, b, [ahead[c] - shifted(back[c], k, -1) for c in range(6)])
            return carry

        lax.fori_loop(0, depth * n_block, xy_body, 0)

    def z_planes(z, b, above, below):
        link = links_at(2, z)
        ahead = colour_rows(link, above, False)
        put_kets(2, z, b, [ahead[c] - below[c] for c in range(6)])

    def own_back(z, b):
        return colour_rows(links_at(2, z), [own(z, c, b) for c in range(6)], True)

    def mid_body(t, carry):
        z = t // n_block + 1
        b = t % n_block
        above = [own(z + 1, c, b) for c in range(6)]
        z_planes(z, b, above, own_back(z - 1, b))
        return carry

    lax.fori_loop(0, (depth - 2) * n_block, mid_body, 0)

    load_s.wait()
    load_p.wait()
    half = s_ref.shape[1]
    for part in range(2):
        def st_body(cb, carry, part=part):
            c_at = pl.multiple_of(cb * 128, 128)
            for kb in range(half // 128):
                tile = s_vm[part, kb * 128:(kb + 1) * 128, pl.ds(c_at, 128)].T
                hi, lo = split(tile)
                cols = slice(part * half + kb * 128, part * half + (kb + 1) * 128)
                st_hi[pl.ds(c_at, 128), cols] = hi
                st_lo[pl.ds(c_at, 128), cols] = lo
            return carry

        lax.fori_loop(0, half // 128, st_body, 0)
    weight = jnp.where(ins_ref[0] < sink_ref[0], 1.0, 0.0).astype(F32)
    rows = p_ref.shape[1]
    for spin in range(NSPIN):
        scale = weight if spin < 2 else -weight
        re = p_vm[0, :, spin * nv:(spin + 1) * nv] * scale
        im = p_vm[1, :, spin * nv:(spin + 1) * nv] * scale
        for row, col, val in ((0, 0, re), (0, 1, -im), (1, 0, im), (1, 1, re)):
            hi, lo = split(val)
            p2_hi[spin, row * rows:(row + 1) * rows, col * nv:(col + 1) * nv] = hi
            p2_lo[spin, row * rows:(row + 1) * rows, col * nv:(col + 1) * nv] = lo

    def elemental(z):
        for copy in bra_copies[z]:
            copy.wait_recv()
        for c in range(3):
            re_hi, re_lo = split(bra[z, c])
            im_hi, im_lo = split(bra[z, 3 + c])
            for ref, re, im in ((rhs_hi, re_hi, im_hi), (rhs_lo, re_lo, im_lo)):
                left_cols = slice(c * plane, (c + 1) * plane)
                right_cols = slice((3 + c) * plane, (4 + c) * plane)
                ref[0:nv, left_cols] = re
                ref[0:nv, right_cols] = im
                ref[nv:2 * nv, left_cols] = -im
                ref[nv:2 * nv, right_cols] = re
        part = dot3(ket_hi[z], ket_lo[z], rhs_hi[...], rhs_lo[...], NT).reshape(acc.shape)
        if z == order[0]:
            acc[...] = part
        else:
            acc[...] += part

    for z in order[:-2]:
        elemental(z)

    halo_w.wait()

    def low_body(b, carry):
        above = [own(1, c, b) for c in range(6)]
        z_planes(0, b, above, [halo_dn[c, rows_of(b), :] for c in range(6)])
        return carry

    lax.fori_loop(0, n_block, low_body, 0)
    halo_v.wait()

    def high_body(b, carry):
        above = [halo_up[c, rows_of(b), :] for c in range(6)]
        z_planes(depth - 1, b, above, own_back(depth - 2, b))
        return carry

    lax.fori_loop(0, n_block, high_body, 0)
    for z in order[-2:]:
        elemental(z)

    for m in range(n_mom):
        for e in range(n_dir):
            for part in range(2):
                epart[2 * (m * n_dir + e) + part] = acc[
                    m * n_dir + dir_ref[e], :, part * nv:(part + 1) * nv]

    n_group = pairs2 // n_sp
    per_group = n_sp // 2

    def rs_copy(g, d):
        peer = (me_z + d) % n_sp
        return remote(epart.at[g * n_sp + peer], rs_buf.at[g, d - 1], rs_s.at[g, d - 1],
                      rs_r.at[g, d - 1], "space", peer)

    def ag_copy(g, d):
        return remote(e_own.at[g], e_full.at[g * n_sp + me_z, my_rows, :], ag_s.at[g, d - 1],
                      ag_r.at[g, d - 1], "space", (me_z + d) % n_sp)

    def fx_copy(g, slot, d):
        owner = (me_z + n_sp - slot) % n_sp
        target = e_full.at[g * n_sp + owner, my_rows, :]
        return remote(target if slot else e_own.at[g], target, fx_s.at[g, slot, d - 1],
                      fx_r.at[g, slot, d - 1], "tsink", (me_x + d) % n_ts)

    def reduce(g):
        total = epart[g * n_sp + me_z]
        for d in range(1, n_sp):
            rs_copy(g, d).wait_recv()
            total = total + rs_buf[g, d - 1]
        e_own[g] = total
        e_full[g * n_sp + me_z, my_rows, :] = total
        for d in range(1, n_sp):
            ag_copy(g, d).start()
        for d in range(1, n_ts):
            fx_copy(g, 0, d).start()

    def forward(g):
        for slot in range(1, n_sp):
            ag_copy(g, slot).wait_recv()
            for d in range(1, n_ts):
                fx_copy(g, slot, d).start()

    def left(g):
        for slot in range(n_sp):
            for d in range(1, n_ts):
                fx_copy(g, slot, d).wait_recv()
        for i in range(per_group):
            for part in range(2):
                hi, lo = split(e_full[g * n_sp + 2 * i + part])
                e_hi[i * nv:(i + 1) * nv, part * nv:(part + 1) * nv] = hi
                e_lo[i * nv:(i + 1) * nv, part * nv:(part + 1) * nv] = lo

        def left_body(spin, carry):
            prod = dot3(e_hi[...], e_lo[...], p2_hi[spin], p2_lo[spin], NT)
            at = pl.ds(pl.multiple_of(spin * nv, nv), nv)
            at_low = pl.ds(pl.multiple_of(half + spin * nv, nv), nv)
            for i in range(per_group):
                hi, lo = split(prod[i * nv:(i + 1) * nv])
                for ref, val in ((l2_hi, hi), (l2_lo, lo)):
                    ref[g * per_group + i, at, :] = val
                    ref[g * per_group + i, at_low, 0:rows] = -val[:, rows:]
                    ref[g * per_group + i, at_low, rows:] = val[:, :rows]
            return carry

        lax.fori_loop(0, NSPIN, left_body, 0)

    def spread(g):
        for d in range(1, n_sp):
            rs_copy(g, d).start()

    for g in range(n_group):
        spread(g)
    n_col = recv_a.shape[1]

    def right(q, pair):
        at = pl.ds(pl.multiple_of(pair * (2 * n_col), 2 * n_col), 2 * n_col)
        return dot3(st_hi[at, :], st_lo[at, :], l2_hi[q], l2_lo[q], NN)

    def copy_a(q):
        return remote(tmp_a.at[q, 1 - core], recv_a.at[q], a_s.at[q], a_r.at[q], "tins", mate)

    def copy_y(q):
        return remote(sum_a.at[q], recv_y.at[q], y_s.at[q], y_r.at[q], "tins", far)

    def copy_b(q):
        return remote(tmp_b.at[q, 1 - core], recv_b.at[q], b_s.at[q], b_r.at[q], "tins", mate)

    def relay(q):
        copy_a(q).wait_recv()
        sum_a[q] = tmp_a[q, core] + recv_a[q]
        copy_y(q).start()

    my_pair = me_t // 2

    def near(q):
        res = right(q, 1 - my_pair)
        tmp_a[q, 0] = res[:n_col]
        tmp_a[q, 1] = res[n_col:]
        copy_a(q).start()

    for g in range(n_group + 2):
        if g < n_group:
            reduce(g)
        if 1 <= g <= n_group:
            forward(g - 1)
        if g >= 2:
            left(g - 2)
            for q in range((g - 2) * per_group, (g - 1) * per_group):
                near(q)
                if q:
                    relay(q - 1)
    relay(pairs - 1)
    for q in range(pairs):
        res = right(q, my_pair)
        tmp_b[q, 0] = res[:n_col]
        tmp_b[q, 1] = res[n_col:]
        copy_b(q).start()
    for q in range(pairs):
        copy_b(q).wait_recv()
        copy_y(q).wait_recv()
        val = tmp_b[q, core] + recv_b[q] + recv_y[q]
        for part in range(2):
            out_ref[pl.ds(2 * q + part, n_col, stride=pairs2), :] = (
                val[:, part * rows:(part + 1) * rows])

    for z in order:
        for copy in bra_copies[z]:
            copy.wait_send()
    for g in range(n_group):
        for d in range(1, n_sp):
            rs_copy(g, d).wait_send()
            ag_copy(g, d).wait_send()
        for slot in range(n_sp):
            for d in range(1, n_ts):
                fx_copy(g, slot, d).wait_send()
    for q in range(pairs):
        copy_a(q).wait_send()
        copy_y(q).wait_send()
        copy_b(q).wait_send()


def pair_kernel(
    n_sp, dir_ref, mom_ref, ins_ref, sink_ref, ev_ref, link_hbm, p_ref, s_ref, out_ref,
    link_ref, cos_ref, sin_ref, p_vm, s_vm, in_sem,
    vec_own, vec_far, w_top, halo_up, halo_dn, ket_hi, ket_lo, rhs_own, rhs_far, acc_own, acc_far,
    part_own, part_far, buf_own, buf_far, sum_own, sum_far, e_full, e_two, st_two,
    p2_hi, p2_lo, l2_hi, l2_lo, tmp_a, recv_a, sum_a, tmp_b, recv_b, recv_y,
    loc_sem, v_s, v_r, halo_s, halo_r, rd_s, rd_r, gd_s, gd_r, xd_s, xd_r,
    rf_s, rf_r, gf_s, gf_r, xf_s, xf_r, a_s, a_r, y_s, y_r, b_s, b_r,
):
    _, vecs, depth, plane = ev_ref.shape
    pairs = part_own.shape[1]
    n_dir = 3
    n_mom = pairs // n_dir
    nv = 2 * vecs
    me_x = lax.axis_index("tsink")
    me_z = lax.axis_index("space")
    me_t = lax.axis_index("tins")
    core = me_t % 2
    mate = me_t + 1 - 2 * core
    far = (me_t + 2) % 4
    up = (me_z + 1) % n_sp
    down = (me_z + n_sp - 1) % n_sp
    other = 1 - me_x
    is_head = me_x == core
    not_head = me_x != core

    barrier = pltpu.get_barrier_semaphore()
    mesh_type = pl.DeviceIdType.MESH
    pl.semaphore_signal(barrier, inc=1, device_id={"tsink": other}, device_id_type=mesh_type)
    for d in range(1, n_sp):
        pl.semaphore_signal(barrier, inc=1, device_id={"space": (me_z + d) % n_sp},
                            device_id_type=mesh_type)
    for target in (mate, far):
        pl.semaphore_signal(barrier, inc=1, device_id={"tins": target}, device_id_type=mesh_type)
    local = [
        pltpu.make_async_copy(ev_ref.at[:, :, z, :], vec_own.at[z], loc_sem.at[z])
        for z in range(depth)
    ]
    local[depth - 1].start()
    load_links = pltpu.make_async_copy(link_hbm, link_ref, in_sem.at[2])
    load_links.start()
    for copy in local[:-1]:
        copy.start()
    load_p = pltpu.make_async_copy(p_ref, p_vm, in_sem.at[0])
    load_s = pltpu.make_async_copy(s_ref, s_vm, in_sem.at[1])
    order = list(range(1, depth - 1)) + [0, depth - 1]
    vec_copies = {
        z: remote(ev_ref.at[:, :, z, :], vec_far.at[z], v_s.at[z], v_r.at[z], "tsink", other)
        for z in order
    }
    halo_v = remote(ev_ref.at[:, :, 0, :], halo_up, halo_s.at[0], halo_r.at[0], "space", down)
    halo_w = remote(w_top, halo_dn, halo_s.at[1], halo_r.at[1], "space", up)

    block = min(16, vecs)
    n_block = vecs // block

    def rows_of(b):
        return pl.ds(pl.multiple_of(b * block, block), block)

    def own(z, c, b):
        return vec_own[z, c, rows_of(b), :]

    def links_at(k, z):
        return [
            [[link_ref[k, part, i, j, pl.ds(z, 1), :] for j in range(3)] for i in range(3)]
            for part in range(2)
        ]

    column = lax.broadcasted_iota(jnp.int32, (block, plane), 1) % L

    def shifted(x, k, sign):
        if k == 1:
            return pltpu.roll(x, plane - L if sign > 0 else L, axis=1)
        if sign > 0:
            return jnp.where(column == L - 1, pltpu.roll(x, L - 1, axis=1),
                             pltpu.roll(x, plane - 1, axis=1))
        return jnp.where(column == 0, pltpu.roll(x, plane + 1 - L, axis=1),
                         pltpu.roll(x, 1, axis=1))

    site = lax.broadcasted_iota(jnp.int32, (depth, plane), 1)
    z_coord = me_z * depth + lax.broadcasted_iota(jnp.int32, (depth, plane), 0)
    for m in range(n_mom):
        product = mom_ref[m, 0] * (site % L) + mom_ref[m, 1] * (site // L) + mom_ref[m, 2] * z_coord
        steps = [0] + [mom_ref[m, k] for k in range(n_dir)] + [-mom_ref[m, k] for k in range(n_dir)]
        for j, step in enumerate(steps):
            angles = (2.0 * math.pi / L) * jnp.bitwise_and(product + step, L - 1).astype(F32)
            cos_ref[m, j] = jnp.cos(angles)
            sin_ref[m, j] = jnp.sin(angles)

    def put_kets(k, z, b, ahead, back, turned):
        deriv = [ahead[c] - back[c] for c in range(6)]

        def put(start, i, re, im):
            at = pl.multiple_of(start * vecs + b * block, block)
            for comp, val in ((i, re), (3 + i, im)):
                hi, lo = split(val)
                cols = slice(comp * plane, (comp + 1) * plane)
                ket_hi[z, pl.ds(at, block), cols] = hi
                ket_lo[z, pl.ds(at, block), cols] = lo

        for m in range(n_mom):
            c, c_up, c_dn = [cos_ref[m, j, pl.ds(z, 1), :] for j in (0, 1 + k, 1 + n_dir + k)]
            s, s_up, s_dn = [sin_ref[m, j, pl.ds(z, 1), :] for j in (0, 1 + k, 1 + n_dir + k)]
            for i in range(3):
                put(m * n_dir + k, i, c * deriv[i] + s * deriv[3 + i],
                    c * deriv[3 + i] - s * deriv[i])
                if not turned:
                    continue
                re = c_up * ahead[i] - s_up * ahead[3 + i]
                im = c_up * ahead[3 + i] + s_up * ahead[i]
                if turned == 2:
                    re = re - c_dn * back[i] + s_dn * back[3 + i]
                    im = im - c_dn * back[3 + i] - s_dn * back[i]
                put(pairs + m * n_dir + k, i, re, im)

    def by_role(count, body, head_turned, turned):
        @pl.when(is_head)
        def _():
            lax.fori_loop(0, count, functools.partial(body, head_turned), 0)

        @pl.when(not_head)
        def _():
            lax.fori_loop(0, count, functools.partial(body, turned), 0)

    pl.semaphore_wait(barrier, 1 + n_sp - 1 + 2)

    @pl.when(is_head)
    def _():
        halo_v.start()

    @pl.when(not_head)
    def _():
        for z in order:
            vec_copies[z].start()
        halo_dn[...] = jnp.zeros_like(halo_dn)

    load_links.wait()
    local[depth - 1].wait()

    def top_body(b, carry):
        vec = [own(depth - 1, c, b) for c in range(6)]
        w = colour_rows(links_at(2, depth - 1), vec, True)
        for c in range(6):
            w_top[c, rows_of(b), :] = w[c]
        return carry

    @pl.when(is_head)
    def _():
        lax.fori_loop(0, n_block, top_body, 0)
        halo_w.start()

    @pl.when(not_head)
    def _():
        halo_v.start()

    for copy in local[:-1]:
        copy.wait()
    load_p.start()
    load_s.start()

    for k in range(2):
        def xy_body(turned, t, carry, k=k):
            z = t // n_block
            b = t % n_block
            vec = [own(z, c, b) for c in range(6)]
            link = links_at(k, z)
            ahead = colour_rows(link, [shifted(x, k, 1) for x in vec], False)
            back = colour_rows(link, vec, True)
            put_kets(k, z, b, ahead, [shifted(x, k, -1) for x in back], turned)
            return carry

        by_role(depth * n_block, xy_body, 2, 0)

    def z_planes(z, b, above, below, turned):
        put_kets(2, z, b, colour_rows(links_at(2, z), above, False), below, turned)

    def own_back(z, b):
        return colour_rows(links_at(2, z), [own(z, c, b) for c in range(6)], True)

    def mid_body(turned, t, carry):
        z = t // n_block + 1
        b = t % n_block
        z_planes(z, b, [own(z + 1, c, b) for c in range(6)], own_back(z - 1, b),
                 turned)
        return carry

    by_role((depth - 2) * n_block, mid_body, 2, 0)

    def fill(rhs, vec, z):
        for c in range(3):
            left_cols = slice(c * plane, (c + 1) * plane)
            right_cols = slice((3 + c) * plane, (4 + c) * plane)
            for at, re, im in zip((0, nv), split(vec[z, c]), split(vec[z, 3 + c])):
                rhs[at:at + vecs, left_cols] = re
                rhs[at:at + vecs, right_cols] = im
                rhs[at + vecs:at + nv, left_cols] = -im
                rhs[at + vecs:at + nv, right_cols] = re

    def elemental(z, rhs, acc, start):
        rows = pairs * vecs
        both = lax.dot_general(ket_hi[z, start:start + rows, :], rhs[...], NT,
                               preferred_element_type=F32)
        low = lax.dot_general(ket_lo[z, start:start + rows, :], rhs[0:nv, :], NT,
                              preferred_element_type=F32)
        part = (both[:, :nv] + both[:, nv:] + low).reshape(pairs, vecs, nv)
        at = slice(start // vecs, start // vecs + pairs)
        if z == order[0]:
            acc[at] = part
        else:
            acc[at] += part

    def own_elemental(z):
        fill(rhs_own, vec_own, z)
        elemental(z, rhs_own, acc_own, 0)

    def far_elemental(z):
        @pl.when(is_head)
        def _():
            vec_copies[z].wait_recv()
            fill(rhs_far, vec_far, z)
            for start in (0, pairs * vecs):
                elemental(z, rhs_far, acc_far, start)

    for z in order[:-2]:
        own_elemental(z)

    load_s.wait()
    load_p.wait()
    half = s_ref.shape[1]
    wide = half // 2
    for part in range(2):
        def st_body(cb, carry, part=part):
            c_at = pl.multiple_of(cb * 128, 128)
            for kb in range(half // nv):
                near_at = pl.multiple_of(kb * nv + core * vecs, vecs)
                far_at = pl.multiple_of(kb * nv + (1 - core) * vecs, vecs)
                tile = jnp.concatenate([s_vm[part, pl.ds(near_at, vecs), pl.ds(c_at, 128)],
                                        s_vm[part, pl.ds(far_at, vecs), pl.ds(c_at, 128)]], axis=0).T
                hi, lo = split(tile)
                cols = slice(part * half + kb * nv, part * half + (kb + 1) * nv)
                at = pl.multiple_of(cb // 2 * (2 * wide) + cb % 2 * 128, 128)
                st_two[pl.ds(at, 128), cols] = hi
                st_two[pl.ds(at + wide, 128), cols] = lo
            return carry

        lax.fori_loop(0, half // 128, st_body, 0)
    weight = jnp.where(ins_ref[0] < sink_ref[0], 1.0, 0.0).astype(F32)
    rows = p_ref.shape[1]
    low_lane = lax.broadcasted_iota(jnp.int32, (rows, nv), 1) < vecs
    for spin in range(NSPIN):
        scale = weight if spin < 2 else -weight
        re = p_vm[0, :, spin * nv:(spin + 1) * nv] * scale
        im = p_vm[1, :, spin * nv:(spin + 1) * nv] * scale
        re_roll = pltpu.roll(re, vecs, axis=1)
        im_roll = pltpu.roll(im, vecs, axis=1)
        re, re_roll = jnp.where(core == 0, re, re_roll), jnp.where(core == 0, re_roll, re)
        im, im_roll = jnp.where(core == 0, im, im_roll), jnp.where(core == 0, im_roll, im)
        for row, (x, x_roll, y, y_roll) in enumerate(((re, re_roll, -im, -im_roll),
                                                      (im, im_roll, re, re_roll))):
            for col, val in enumerate((jnp.where(low_lane, x, y_roll), jnp.where(low_lane, x_roll, y))):
                hi, lo = split(val)
                p2_hi[spin, row * rows:(row + 1) * rows, col * nv:(col + 1) * nv] = hi
                p2_lo[spin, row * rows:(row + 1) * rows, col * nv:(col + 1) * nv] = lo

    far_elemental(order[0])
    halo_v.wait()

    def high_body(turned, b, carry):
        above = [halo_up[c, rows_of(b), :] for c in range(6)]
        z_planes(depth - 1, b, above, own_back(depth - 2, b), turned)
        return carry

    by_role(n_block, high_body, 2, 1)
    own_elemental(depth - 1)

    def turn(val):
        flat = val.T
        return jnp.concatenate([-flat[:vecs], flat[vecs:]], axis=1)

    @pl.when(not_head)
    def _():
        for m in range(n_mom):
            q = m * n_dir + n_dir - 1
            at = slice((pairs + q) * vecs, (pairs + q + 1) * vecs)
            both = lax.dot_general(ket_hi[depth - 1, at, :], rhs_own[...], NT,
                                   preferred_element_type=F32)
            low = lax.dot_general(ket_lo[depth - 1, at, :], rhs_own[0:nv, :], NT,
                                  preferred_element_type=F32)
            acc_own[q] += turn(both[:, :nv] + both[:, nv:] + low)

    @pl.when(is_head)
    def _():
        halo_w.wait()

    def low_body(turned, b, carry):
        above = [own(1, c, b) for c in range(6)]
        z_planes(0, b, above, [halo_dn[c, rows_of(b), :] for c in range(6)], turned)
        return carry

    by_role(n_block, low_body, 2, 0)
    own_elemental(0)

    strip = vecs // n_sp
    per_group = part_far.shape[2]
    n_group = pairs // per_group
    my_strip = pl.ds(pl.multiple_of(me_z * strip, strip), strip)
    corner = jnp.where(is_head, 0, 3)

    def chosen(acc, q, base):
        return acc[base + (q // n_dir) * n_dir + dir_ref[q % n_dir]]

    def strips(val):
        return [val[z * strip:(z + 1) * strip, :] for z in range(n_sp)]

    for q in range(pairs):
        for z, val in enumerate(strips(chosen(acc_own, q, 0))):
            part_own[z, q] = val

    def rd_copy(d):
        peer = (me_z + d) % n_sp
        return remote(part_own.at[peer], buf_own.at[d - 1], rd_s.at[d - 1], rd_r.at[d - 1],
                      "space", peer)

    def gd_copy(d):
        return remote(sum_own, e_full.at[:, corner, my_strip, :], gd_s.at[d - 1], gd_r.at[d - 1],
                      "space", (me_z + d) % n_sp)

    def xd_copy(g):
        block_at = e_full.at[pl.ds(g * per_group, per_group), corner]
        return remote(block_at, block_at, xd_s.at[g], xd_r.at[g], "tsink", other)

    def rf_copy(g, d):
        peer = (me_z + d) % n_sp
        return remote(part_far.at[g, peer], buf_far.at[g, d - 1], rf_s.at[g, d - 1],
                      rf_r.at[g, d - 1], "space", peer)

    def mixed(g, strip_at):
        return e_full.at[pl.ds(g * per_group, per_group), pl.ds(1, 2), strip_at, :]

    def gf_copy(g, d):
        return remote(sum_far.at[g], mixed(g, my_strip), gf_s.at[g, d - 1], gf_r.at[g, d - 1],
                      "space", (me_z + d) % n_sp)

    def xf_copy(g, slot):
        return pltpu.make_async_remote_copy(
            src_ref=sum_far.at[g], dst_ref=mixed(g, my_strip), send_sem=xf_s.at[g, slot],
            recv_sem=xf_r.at[g, slot], device_id={"tsink": other, "space": (me_z + slot) % n_sp},
            device_id_type=pl.DeviceIdType.MESH)

    for d in range(1, n_sp):
        rd_copy(d).start()
    for z in order[1:-1]:
        far_elemental(z)
    total = part_own[me_z]
    for d in range(1, n_sp):
        rd_copy(d).wait_recv()
        total = total + buf_own[d - 1]
    sum_own[...] = total
    e_full[:, corner, my_strip, :] = total
    for d in range(1, n_sp):
        gd_copy(d).start()
    far_elemental(order[-1])

    @pl.when(is_head)
    def _():
        for q in range(pairs):
            g, i = q // per_group, q % per_group
            for z, val in enumerate(strips(chosen(acc_far, q, 0))):
                part_far[g, z, i, 0] = val
            for z, val in enumerate(strips(turn(chosen(acc_far, q, pairs)))):
                part_far[g, z, i, 1] = val
            if i == per_group - 1:
                for d in range(1, n_sp):
                    rf_copy(g, d).start()

    @pl.when(not_head)
    def _():
        for z in order:
            vec_copies[z].wait_send()

    def reduce(g):
        @pl.when(is_head)
        def _():
            total = part_far[g, me_z]
            for d in range(1, n_sp):
                rf_copy(g, d).wait_recv()
                total = total + buf_far[g, d - 1]
            sum_far[g] = total
            e_full[pl.ds(g * per_group, per_group), pl.ds(1, 2), my_strip, :] = total
            for d in range(1, n_sp):
                gf_copy(g, d).start()
            for slot in range(n_sp):
                xf_copy(g, slot).start()

    def forward(g):
        @pl.when(is_head)
        def _():
            for d in range(1, n_sp):
                gf_copy(g, d).wait_recv()

    def left(g):
        xd_copy(g).wait_recv()

        @pl.when(not_head)
        def _():
            for slot in range(n_sp):
                xf_copy(g, slot).wait_recv()

        for i in range(per_group):
            for quad in range(4):
                hi, lo = split(e_full[g * per_group + i, quad])
                at = i * nv + quad // 2 * vecs
                low_at = at + per_group * nv
                cols = slice(quad % 2 * nv, (quad % 2 + 1) * nv)
                e_two[at:at + vecs, cols] = hi
                e_two[low_at:low_at + vecs, cols] = lo

        def left_body(spin, carry):
            prod = dot_two(e_two[...], p2_hi[spin], p2_lo[spin], NT)
            at = pl.ds(pl.multiple_of(spin * nv, nv), nv)
            at_low = pl.ds(pl.multiple_of(half + spin * nv, nv), nv)
            for i in range(per_group):
                hi, lo = split(prod[i * nv:(i + 1) * nv])
                for ref, val in ((l2_hi, hi), (l2_lo, lo)):
                    ref[g * per_group + i, at, :] = val
                    ref[g * per_group + i, at_low, 0:rows] = -val[:, rows:]
                    ref[g * per_group + i, at_low, rows:] = val[:, :rows]
            return carry

        lax.fori_loop(0, NSPIN, left_body, 0)

    n_col = recv_a.shape[1]

    def right(q, pair):
        at = pl.ds(pl.multiple_of(pair * (2 * wide), 2 * wide), 2 * wide)
        return dot_two(st_two[at, :], l2_hi[q], l2_lo[q], NN)

    def copy_a(q):
        return remote(tmp_a.at[q, 1 - core], recv_a.at[q], a_s.at[q], a_r.at[q], "tins", mate)

    def copy_y(q):
        return remote(sum_a.at[q], recv_y.at[q], y_s.at[q], y_r.at[q], "tins", far)

    def copy_b(q):
        return remote(tmp_b.at[q, 1 - core], recv_b.at[q], b_s.at[q], b_r.at[q], "tins", mate)

    def relay(q):
        copy_a(q).wait_recv()
        sum_a[q] = tmp_a[q, core] + recv_a[q]
        copy_y(q).start()

    my_pair = me_t // 2

    def near(q):
        res = right(q, 1 - my_pair)
        tmp_a[q, 0] = res[:n_col]
        tmp_a[q, 1] = res[n_col:]
        copy_a(q).start()

    ahead = min(2, n_group)

    def spread_own():
        for d in range(1, n_sp):
            gd_copy(d).wait_recv()
        for h in range(n_group):
            xd_copy(h).start()

    for g in range(ahead):
        if g == 1:
            spread_own()
        reduce(g)
    for g in range(n_group):
        if g + ahead < n_group:
            reduce(g + ahead)
        forward(g)
        left(g)
        for q in range(g * per_group, (g + 1) * per_group):
            if q:
                relay(q - 1)
            near(q)
    for q in range(pairs):
        res = right(q, my_pair)
        if q == 0:
            relay(pairs - 1)
        tmp_b[q, 0] = res[:n_col]
        tmp_b[q, 1] = res[n_col:]
        copy_b(q).start()
    for q in range(pairs):
        copy_b(q).wait_recv()
        copy_y(q).wait_recv()
        val = tmp_b[q, core] + recv_b[q] + recv_y[q]
        for part in range(2):
            out_ref[pl.ds(2 * q + part, n_col, stride=2 * pairs), :] = (
                val[:, part * rows:(part + 1) * rows])

    for d in range(1, n_sp):
        rd_copy(d).wait_send()
        gd_copy(d).wait_send()

    @pl.when(is_head)
    def _():
        for g in range(n_group):
            for d in range(1, n_sp):
                rf_copy(g, d).wait_send()
                gf_copy(g, d).wait_send()
            for slot in range(n_sp):
                xf_copy(g, slot).wait_send()

    for g in range(n_group):
        xd_copy(g).wait_send()
    for q in range(pairs):
        copy_a(q).wait_send()
        copy_y(q).wait_send()
        copy_b(q).wait_send()


def copy_kernel(in_ref, out_ref):
    out_ref[...] = in_ref[...]


def ring_call(n_ts, n_sp, n_ti, eigvecs, links, momenta, directions, ins_time, sink_time,
              sink_peramb, source_peramb):
    assert n_ti == 4
    _, _, _, vecs, depth, plane = eigvecs.shape
    nv = vecs * n_ts
    ev = eigvecs.reshape(6, vecs, depth, plane)
    pairs = momenta.shape[0] * directions.shape[0]
    order_m = source_peramb.shape[-1]
    rows = sink_peramb.shape[3]
    n_col = order_m // n_ti
    n_group = 2 * pairs // n_sp
    v = pltpu.VMEM
    dma = pltpu.SemaphoreType.DMA
    scratch = [
        v((momenta.shape[0], depth, plane), F32), v((momenta.shape[0], depth, plane), F32),
        v(sink_peramb.shape[2:], F32), v(source_peramb.shape[1:], F32), dma((2,)),
        v((depth, 6, nv, plane), F32),
        v((6, vecs, plane), F32), v((6, vecs, plane), F32), v((6, vecs, plane), F32),
        v((depth, pairs * vecs, 6 * plane), BF16), v((depth, pairs * vecs, 6 * plane), BF16),
        v((2 * nv, 6 * plane), BF16), v((2 * nv, 6 * plane), BF16),
        v((pairs, vecs, 2 * nv), F32),
        v((2 * pairs, vecs, nv), F32),
        v((n_group, n_sp - 1, vecs, nv), F32),
        v((n_group, vecs, nv), F32),
        v((2 * pairs, nv, nv), F32),
        v((n_sp // 2 * nv, 2 * nv), BF16), v((n_sp // 2 * nv, 2 * nv), BF16),
        v((order_m, 2 * order_m), BF16), v((order_m, 2 * order_m), BF16),
        v((NSPIN, 2 * rows, 2 * nv), BF16), v((NSPIN, 2 * rows, 2 * nv), BF16),
        v((pairs, 2 * order_m, 2 * rows), BF16), v((pairs, 2 * order_m, 2 * rows), BF16),
        v((pairs, 2, n_col, 2 * rows), F32),
        v((pairs, n_col, 2 * rows), F32), v((pairs, n_col, 2 * rows), F32),
        v((pairs, 2, n_col, 2 * rows), F32),
        v((pairs, n_col, 2 * rows), F32), v((pairs, n_col, 2 * rows), F32),
        dma((depth,)), dma((depth, n_ts - 1)), dma((depth, n_ts - 1)), dma((2,)), dma((2,)),
        dma((n_group, n_sp - 1)), dma((n_group, n_sp - 1)),
        dma((n_group, n_sp - 1)), dma((n_group, n_sp - 1)),
        dma((n_group, n_sp, n_ts - 1)), dma((n_group, n_sp, n_ts - 1)),
        dma((pairs,)), dma((pairs,)), dma((pairs,)), dma((pairs,)), dma((pairs,)), dma((pairs,)),
    ]
    smem = pl.BlockSpec(memory_space=pltpu.SMEM)
    vmem = pl.BlockSpec(memory_space=pltpu.VMEM)
    hbm = pl.BlockSpec(memory_space=pl.ANY)
    out = pl.pallas_call(
        functools.partial(ring_kernel, n_ts, n_sp),
        out_shape=jax.ShapeDtypeStruct((n_col * pairs * 2, rows), F32),
        in_specs=[smem] * 4 + [hbm, vmem, hbm, hbm],
        out_specs=vmem,
        scratch_shapes=scratch,
        compiler_params=pltpu.CompilerParams(
            collective_id=0, has_side_effects=True, vmem_limit_bytes=60 * 1024 * 1024
        ),
        name="peramb",
    )(directions, momenta, ins_time, sink_time, ev, links[0], sink_peramb[0, 0],
      source_peramb[0])
    tile = pl.BlockSpec((out.shape[0] // 2, rows), lambda i: (i, 0))
    out = pl.pallas_call(
        copy_kernel,
        grid=(2,),
        out_shape=jax.ShapeDtypeStruct(out.shape, F32),
        in_specs=[tile],
        out_specs=tile,
        name="result",
    )(out)
    return out.reshape(n_col, 1, pairs, 2, rows)


def pair_call(n_ts, n_sp, n_ti, eigvecs, links, momenta, directions, ins_time, sink_time,
              sink_peramb, source_peramb):
    assert n_ts == 2 and n_ti == 4
    _, _, _, vecs, depth, plane = eigvecs.shape
    nv = vecs * n_ts
    ev = eigvecs.reshape(6, vecs, depth, plane)
    n_mom = momenta.shape[0]
    pairs = n_mom * directions.shape[0]
    order_m = source_peramb.shape[-1]
    rows = sink_peramb.shape[3]
    n_col = order_m // n_ti
    per_group = 1
    n_group = pairs // per_group
    strip = vecs // n_sp
    v = pltpu.VMEM
    dma = pltpu.SemaphoreType.DMA
    scratch = [
        v(links.shape[1:], F32), v((n_mom, 7, depth, plane), F32), v((n_mom, 7, depth, plane), F32),
        v(sink_peramb.shape[2:], F32), v(source_peramb.shape[1:], F32), dma((3,)),
        v((depth, 6, vecs, plane), F32), v((depth, 6, vecs, plane), F32),
        v((6, vecs, plane), F32), v((6, vecs, plane), F32), v((6, vecs, plane), F32),
        v((depth, 2 * pairs * vecs, 6 * plane), BF16), v((depth, 2 * pairs * vecs, 6 * plane), BF16),
        v((2 * nv, 6 * plane), BF16), v((2 * nv, 6 * plane), BF16),
        v((pairs, vecs, nv), F32), v((2 * pairs, vecs, nv), F32),
        v((n_sp, pairs, strip, nv), F32), v((n_group, n_sp, per_group, 2, strip, nv), F32),
        v((n_sp - 1, pairs, strip, nv), F32), v((n_group, n_sp - 1, per_group, 2, strip, nv), F32),
        v((pairs, strip, nv), F32), v((n_group, per_group, 2, strip, nv), F32),
        v((pairs, 4, vecs, nv), F32),
        v((2 * per_group * nv, 2 * nv), BF16), v((2 * order_m, 2 * order_m), BF16),
        v((NSPIN, 2 * rows, 2 * nv), BF16), v((NSPIN, 2 * rows, 2 * nv), BF16),
        v((pairs, 2 * order_m, 2 * rows), BF16), v((pairs, 2 * order_m, 2 * rows), BF16),
        v((pairs, 2, n_col, 2 * rows), F32),
        v((pairs, n_col, 2 * rows), F32), v((pairs, n_col, 2 * rows), F32),
        v((pairs, 2, n_col, 2 * rows), F32),
        v((pairs, n_col, 2 * rows), F32), v((pairs, n_col, 2 * rows), F32),
        dma((depth,)), dma((depth,)), dma((depth,)), dma((2,)), dma((2,)),
        dma((n_sp - 1,)), dma((n_sp - 1,)), dma((n_sp - 1,)), dma((n_sp - 1,)),
        dma((n_group,)), dma((n_group,)),
        dma((n_group, n_sp - 1)), dma((n_group, n_sp - 1)),
        dma((n_group, n_sp - 1)), dma((n_group, n_sp - 1)),
        dma((n_group, n_sp)), dma((n_group, n_sp)),
        dma((pairs,)), dma((pairs,)), dma((pairs,)), dma((pairs,)), dma((pairs,)), dma((pairs,)),
    ]
    smem = pl.BlockSpec(memory_space=pltpu.SMEM)
    vmem = pl.BlockSpec(memory_space=pltpu.VMEM)
    hbm = pl.BlockSpec(memory_space=pl.ANY)
    out = pl.pallas_call(
        functools.partial(pair_kernel, n_sp),
        out_shape=jax.ShapeDtypeStruct((n_col * pairs * 2, rows), F32),
        in_specs=[smem] * 4 + [hbm] * 4,
        out_specs=vmem,
        scratch_shapes=scratch,
        compiler_params=pltpu.CompilerParams(
            collective_id=0, has_side_effects=True, vmem_limit_bytes=60 * 1024 * 1024
        ),
        name="peramb",
    )(directions, momenta, ins_time, sink_time, ev, links[0], sink_peramb[0, 0],
      source_peramb[0])
    tile = pl.BlockSpec((out.shape[0] // 2, rows), lambda i: (i, 0))
    out = pl.pallas_call(
        copy_kernel,
        grid=(2,),
        out_shape=jax.ShapeDtypeStruct(out.shape, F32),
        in_specs=[tile],
        out_specs=tile,
        name="result",
    )(out)
    return out.reshape(n_col, 1, pairs, 2, rows)


def solution(mesh):
    in_specs = (
        P("tins", None, None, "tsink", "space", None),
        P("tins", None, None, None, None, "space", None),
        P(),
        P(),
        P("tins"),
        P("tsink"),
        P("tsink", "tins", None, "space", None),
        P("tins", None, None, None),
    )
    out_specs = P("tins", "tsink", None, None, "space")
    sizes = mesh.shape["tsink"], mesh.shape["space"], mesh.shape["tins"]
    body = functools.partial(pair_call if sizes[0] == 2 else ring_call, *sizes)
    return jax.shard_map(body, mesh=mesh, in_specs=in_specs, out_specs=out_specs, check_vma=False)
```
